128 devices in a mesh: chan: 16 (over y_lo, x, core), row: 8 (over y_hi, z).
Axes of the slice: x: 4, y: 4 (y_hi: 2, y_lo: 2; y = y_hi * 2 + y_lo), z: 4, core: 2. Of those that a mesh axis runs over, the one named last changes fastest.
Arguments:
- samples: bfloat16 [8, 128, 65536], P(None, 'chan', 'row'), may hold values from -6 to 6
- history: bfloat16 [8, 128, 7168], P(None, 'chan'), may hold values from -6 to 6
- antenna_flags: int32 [1024], replicated, may hold values 0 or 1
- beam_delays: int32 [256, 1024], replicated, may hold values from 0 to 1023
Outputs:
- visibilities: bfloat16 [512, 2, 1024, 1024], P('chan', None, 'row')
- beam_series: float32 [256, 64, 1024], P(('chan', 'row'))
The draws below stay inside these ranges and needn't reach their ends.
All inputs are finite; a program needn't handle non-finite values.
Results may differ from the reference program's by a relative error of at most 0.0075.
Values may be sent and summed in bfloat16 or wider, within the bound.
A program may use at most 128 MiB of HBM per device.

```python
import math
import jax
import jax.numpy as jnp
from jax import lax

A = 1024
FOURIER_LENGTH = 1024
NCH = 512
FILTER_TAPS = 8
BEAMS = 256
FR = 8
F = 64
N_ROW = 8


def with_ends(values, stream_key, least, high):
    dims = values.shape
    place = [jax.random.randint(jax.random.fold_in(stream_key, axis), (), 0, dims[axis]) for axis in range(len(dims))]
    values = values.at[tuple(place)].set(least)
    longest = dims.index(max(dims))
    place[longest] = (place[longest] + 1) % dims[longest]
    return values.at[tuple(place)].set(high)


def shard_levels(own_key, dims, split, low, high):
    gain = 1.0
    for dim, blocks in split:
        draws = jax.random.uniform(jax.random.fold_in(jax.random.fold_in(own_key, 6), dim), (blocks,), jnp.float32, low / len(split), high / len(split))
        gain = gain * jnp.repeat(jnp.exp(draws), dims[dim] // blocks).reshape((-1,) + (1,) * (len(dims) - 1 - dim))
    return gain


def gaussian(stream_key, extent, deviation, reach, shards=(), kind=jnp.bfloat16):
    level = shard_levels(stream_key, extent, shards, -0.22, 0.18) if shards else 1.0
    values = jax.random.normal(stream_key, extent, jnp.float32) * deviation * level
    return jnp.minimum(jnp.maximum(values, -reach), reach).astype(kind)


def setup_inputs(seed: int = 0) -> dict:
    keys = jax.random.split(jax.random.key(seed), 5)
    return {
        "samples": gaussian(keys[0], (N_ROW, A // N_ROW, F * FOURIER_LENGTH), 1.0, 6.0, ((1, 16), (2, 8))),
        "history": gaussian(keys[1], (N_ROW, A // N_ROW, (FILTER_TAPS - 1) * FOURIER_LENGTH), 1.0, 6.0, ((1, 16),)),
        "antenna_flags": with_ends((jax.random.randint(keys[2], (A,), 0, 8) < 7).astype(jnp.int32), jax.random.fold_in(keys[2], 1), 0, 1),
        "beam_delays": with_ends(jax.random.randint(keys[3], (BEAMS, A), 0, FOURIER_LENGTH), jax.random.fold_in(keys[3], 1), 0, FOURIER_LENGTH - 1).astype(jnp.int32),
    }


def tap_table():
    position = jnp.arange(FILTER_TAPS * FOURIER_LENGTH, dtype=jnp.int32).astype(jnp.float32) + 0.5
    centred = position / FOURIER_LENGTH - FILTER_TAPS / 2.0
    window = 0.5 - 0.5 * jnp.cos(2.0 * math.pi * position / (FILTER_TAPS * FOURIER_LENGTH))
    return (jnp.sinc(centred) * window).reshape(FILTER_TAPS, FOURIER_LENGTH)

def dft_table():
    sample_ids = jnp.arange(FOURIER_LENGTH, dtype=jnp.int32)
    chan_ids = jnp.arange(NCH, dtype=jnp.int32)
    phase_angle = (sample_ids[:, None] * chan_ids[None, :] % FOURIER_LENGTH).astype(jnp.float32) * (2.0 * math.pi / FOURIER_LENGTH)
    scale = 1.0 / math.sqrt(FOURIER_LENGTH)
    return jnp.stack([jnp.cos(phase_angle) * scale, -jnp.sin(phase_angle) * scale], axis=1).astype(jnp.bfloat16)

def synth_table():
    chan_ids = jnp.arange(NCH, dtype=jnp.int32)
    sample_ids = jnp.arange(FOURIER_LENGTH, dtype=jnp.int32)
    phase_angle = (chan_ids[:, None] * sample_ids[None, :] % FOURIER_LENGTH).astype(jnp.float32) * (2.0 * math.pi / FOURIER_LENGTH)
    scale = 1.0 / math.sqrt(NCH)
    return jnp.stack([jnp.cos(phase_angle) * scale, -jnp.sin(phase_angle) * scale], axis=0).astype(jnp.bfloat16)

def steering(delay_rows, chan_ids):
    delay_index = delay_rows[None, :, :] * chan_ids[:, None, None] % FOURIER_LENGTH
    phase_angle = delay_index.astype(jnp.float32) * (2.0 * math.pi / FOURIER_LENGTH)
    scale = 1.0 / math.sqrt(A)
    return ((jnp.cos(phase_angle) * scale).astype(jnp.bfloat16), (-jnp.sin(phase_angle) * scale).astype(jnp.bfloat16))

def reference(samples, history, antenna_flags, beam_delays):
    frames = FR * N_ROW
    antenna_samples = samples.reshape(A, frames * FOURIER_LENGTH)
    earlier = history.reshape(A, (FILTER_TAPS - 1) * FOURIER_LENGTH)
    extended = jnp.concatenate([earlier, antenna_samples], axis=1).reshape(A, frames + FILTER_TAPS - 1, FOURIER_LENGTH)
    tap_weights = tap_table()
    filter_output = jnp.zeros((A, frames, FOURIER_LENGTH), jnp.float32)
    for tap in range(FILTER_TAPS):
        filter_output = filter_output + extended[:, tap:tap + frames, :].astype(jnp.float32) * tap_weights[tap]
    filter_output = filter_output.astype(jnp.bfloat16)
    spectra = jnp.dot(filter_output.reshape(A * frames, FOURIER_LENGTH).astype(jnp.float32), dft_table().reshape(FOURIER_LENGTH, 2 * NCH).astype(jnp.float32), preferred_element_type=jnp.float32)
    spectra = spectra.astype(jnp.bfloat16).reshape(A, frames, 2, NCH)
    spectra = spectra * antenna_flags.astype(jnp.bfloat16)[:, None, None, None]
    per_chan = spectra.transpose(3, 0, 2, 1).reshape(NCH, A, 2 * frames)
    chan_ids = jnp.arange(NCH, dtype=jnp.int32)

    def per_channel(chan_item):
        values, chan_index = chan_item
        wide = values.astype(jnp.float32)
        swapped = jnp.concatenate([wide[:, frames:], -wide[:, :frames]], axis=1)
        real_part = jnp.dot(wide, wide.T, preferred_element_type=jnp.float32)
        imag_part = jnp.dot(swapped, wide.T, preferred_element_type=jnp.float32)
        products = (jnp.stack([real_part, imag_part]) / frames).astype(jnp.bfloat16)
        w_real, w_imag = steering(beam_delays, chan_index[None])
        w_real = w_real[0].astype(jnp.float32)
        w_imag = w_imag[0].astype(jnp.float32)
        x_real = wide[:, :frames]
        x_imag = wide[:, frames:]
        beam_real = jnp.dot(w_real, x_real, preferred_element_type=jnp.float32) - jnp.dot(w_imag, x_imag, preferred_element_type=jnp.float32)
        beam_imag = jnp.dot(w_real, x_imag, preferred_element_type=jnp.float32) + jnp.dot(w_imag, x_real, preferred_element_type=jnp.float32)
        return (products, jnp.stack([beam_real, beam_imag]))
    visibilities, beam_spectra = lax.map(per_channel, (per_chan, chan_ids))
    beam_spectra = beam_spectra.transpose(2, 1, 0, 3).astype(jnp.bfloat16)
    beam_series = jnp.einsum('bekf,ekn->bfn', beam_spectra.astype(jnp.float32), synth_table().astype(jnp.float32), preferred_element_type=jnp.float32)
    return (visibilities, beam_series)
```

```python
import math

import jax
import jax.numpy as jnp
import numpy as np
from jax import lax
from jax.experimental import pallas as pl
from jax.experimental.pallas import tpu as pltpu
from jax.sharding import PartitionSpec as P

A = 1024
FL = 1024
NCH = 512
TAPS = 8
BEAMS = 256
NC = 16
NR = 8
CHB = NCH // NC
ROWS = A // NR
AL = ROWS // NC
F = 64
Q = 4
CH = CHB // Q
KK = NC * CH
HALF = CH // 2
HIST = (TAPS - 1) * FL
SPAN = (F // NR) * FL
MESH = pl.DeviceIdType.MESH
F32 = jnp.float32
BF16 = jnp.bfloat16
NKIND = 16


def tap_table():
    position = (np.arange(TAPS * FL, dtype=np.int32).astype(np.float32) + np.float32(0.5)).astype(np.float64)
    centred = position / FL - TAPS / 2.0
    window = 0.5 - 0.5 * np.cos(2.0 * math.pi * position / (TAPS * FL))
    return (np.sinc(centred) * window).reshape(TAPS, FL).astype(np.float32)


def cos_sin(m):
    quarter = lax.shift_right_logical(m, 8)
    x = ((m & 255) - 128).astype(F32) * (2.0 * math.pi / FL)
    x2 = x * x
    s = x * (1.0 + x2 * (-1.0 / 6 + x2 * (1.0 / 120 + x2 * (-1.0 / 5040 + x2 * (1.0 / 362880)))))
    c = 1.0 + x2 * (-0.5 + x2 * (1.0 / 24 + x2 * (-1.0 / 720 + x2 * (1.0 / 40320 + x2 * (-1.0 / 3628800)))))
    root = math.sqrt(0.5)
    ca = (c - s) * root
    sa = (c + s) * root
    odd = (quarter & 1) == 1
    neg = quarter >= 2
    cv = jnp.where(odd, -sa, ca)
    sv = jnp.where(odd, ca, sa)
    return jnp.where(neg, -cv, cv), jnp.where(neg, -sv, sv)


def nt(lhs, rhs):
    return lax.dot_general(lhs, rhs, (((1,), (1,)), ((), ())), preferred_element_type=F32)


def front_kernel(
    samples, history, taps, flags, delays, g_out, series,
    ext, filt32, filt, dftc, dfts, tmp, sbuf, abuf, g, transit, wcos, wall, bs, bsend, z_in, ptab, qtab,
    s_row, r_row, s_loc, s_ch, r_ch, s_g, r_g, s_bm, r_bm, s_out,
):
    c = lax.axis_index("chan")
    r = lax.axis_index("row")
    c_low = lax.rem(c, 8)
    y_lo = c // 8
    h = r // 4
    z = lax.rem(r, 4)
    y = 2 * h + y_lo
    zp = lax.rem(z + 1, 4)
    zm = lax.rem(z + 3, 4)
    z2 = lax.rem(z + 2, 4)
    yp = lax.rem(y + 1, 4)
    ym = lax.rem(y + 3, 4)
    up = {"chan": c, "row": h * 4 + zp}
    dn = {"chan": c, "row": h * 4 + zm}
    fw = {"chan": lax.rem(yp, 2) * 8 + c_low, "row": (yp // 2) * 4 + z}
    bw = {"chan": lax.rem(ym, 2) * 8 + c_low, "row": (ym // 2) * 4 + z}

    def remote(src, dst, ss, rs, dev):
        return pltpu.make_async_remote_copy(
            src_ref=src, dst_ref=dst, send_sem=ss, recv_sem=rs, device_id=dev, device_id_type=MESH
        )

    barrier = pltpu.get_barrier_semaphore()
    for d in range(1, NR):
        pl.semaphore_signal(barrier, inc=1, device_id={"chan": c, "row": lax.rem(r + d, NR)}, device_id_type=MESH)
    for d in range(1, NC):
        pl.semaphore_signal(barrier, inc=1, device_id={"chan": lax.rem(c + d, NC), "row": r}, device_id_type=MESH)
    pl.semaphore_signal(barrier, inc=1, device_id=fw, device_id_type=MESH)
    pl.semaphore_signal(barrier, inc=1, device_id=bw, device_id_type=MESH)
    pl.semaphore_wait(barrier, NR - 1 + NC - 1 + 2)

    def span(row):
        return ext.at[:, pl.ds(pl.multiple_of(HIST + row * SPAN, FL), SPAN)]

    row_sends = []
    for d in range(1, NR):
        to = lax.rem(r + d, NR)
        cp = remote(samples.at[to], span(r), s_row.at[d], r_row.at[d], {"chan": c, "row": to})
        cp.start()
        row_sends.append(cp)
    own = pltpu.make_async_copy(samples.at[r], span(r), s_loc.at[0])
    own.start()
    hist = pltpu.make_async_copy(history.at[r], ext.at[:, pl.ds(0, HIST)], s_loc.at[1])
    hist.start()

    def dft_rows(i, _):
        row = i * 16 + lax.broadcasted_iota(jnp.int32, (16, FL), 0)
        q, rest = row // KK, row % KK
        k = (rest // CH) * CHB + q * CH + rest % CH
        n = lax.broadcasted_iota(jnp.int32, (16, FL), 1)
        cv, sv = cos_sin((k * n) & (FL - 1))
        scale = 1.0 / math.sqrt(FL)
        at = pl.ds(pl.multiple_of(i * 16, 16), 16)
        dftc[at, :] = (cv * scale).astype(BF16)
        dfts[at, :] = (-sv * scale).astype(BF16)
        return 0

    lax.fori_loop(0, NCH // 16, dft_rows, 0)

    def synth_rows(i, _):
        k = i * 16 + lax.broadcasted_iota(jnp.int32, (16, FL), 0)
        n = lax.broadcasted_iota(jnp.int32, (16, FL), 1)
        cv, sv = cos_sin((k * n) & (FL - 1))
        scale = 1.0 / math.sqrt(NCH)
        at = pl.ds(pl.multiple_of(i * 16, 16), 16)
        ptab[at, :] = (cv * scale).astype(BF16)
        qtab[at, :] = (-sv * scale).astype(BF16)
        return 0

    lax.fori_loop(0, NCH // 16, synth_rows, 0)

    for e in range(2):
        for i in range(NC):
            wcos[e * NC + i : e * NC + i + 1, :] = delays[pl.ds(i * 2 * NR + 2 * r + e, 1), :]

    def steer(i, _):
        lanes = pl.ds(pl.multiple_of(i * 128, 128), 128)
        d = wcos[:, lanes]
        cr, ci = cos_sin((d * (c * CHB)) & (FL - 1))
        sr, si = cos_sin(d)
        scale = 1.0 / math.sqrt(A)
        for ch in range(CHB):
            wall[ch, 0:32, lanes] = (cr * scale).astype(BF16)
            wall[ch, 32:64, lanes] = (-ci * scale).astype(BF16)
            cr, ci = cr * sr - ci * si, cr * si + ci * sr
        return 0

    lax.fori_loop(0, A // 128, steer, 0)

    own.wait()
    hist.wait()
    for d in range(1, NR):
        frm = lax.rem(r + NR - d, NR)
        remote(samples.at[frm], span(frm), s_row.at[d], r_row.at[d], {"chan": c, "row": frm}).wait_recv()

    def pfb(i, _):
        lanes = pl.ds(pl.multiple_of(i * 128, 128), 128)
        tap = [jnp.broadcast_to(taps[t : t + 1, lanes], (AL, 128)) for t in range(TAPS)]
        win = [ext[:, pl.ds(pl.multiple_of(t * FL + i * 128, 128), 128)].astype(F32) for t in range(TAPS - 1)]
        for f in range(F):
            win.append(ext[:, pl.ds(pl.multiple_of((f + TAPS - 1) * FL + i * 128, 128), 128)].astype(F32))
            acc = win[f] * tap[0]
            for t in range(1, TAPS):
                acc = acc + win[f + t] * tap[t]
            filt32[f * AL : (f + 1) * AL, :] = acc
        for a in range(AL):
            for b in range(F // 16):
                filt[a * F + b * 16 : a * F + (b + 1) * 16, lanes] = filt32[
                    pl.ds(b * 16 * AL + a, 16, stride=AL), :
                ].astype(BF16)
        return 0

    lax.fori_loop(0, FL // 128, pfb, 0)

    low = lax.broadcasted_iota(jnp.int32, (KK, 128), 1) < 64
    for q in range(Q):
        rows = slice(q * KK, (q + 1) * KK)
        re = nt(dftc[rows, :], filt[...])
        im = nt(dfts[rows, :], filt[...])
        for t in range(AL // 2):
            rt = re[:, t * 128 : (t + 1) * 128]
            it = im[:, t * 128 : (t + 1) * 128]
            tmp[(2 * t) * KK : (2 * t + 1) * KK, :] = jnp.where(low, rt, pltpu.roll(it, 64, 1))
            tmp[(2 * t + 1) * KK : (2 * t + 2) * KK, :] = jnp.where(low, pltpu.roll(rt, 64, 1), it)

        def turn(i, _, q=q):
            for p in range(CH // 2):
                pair = [tmp[pl.ds(i * CH + 2 * p + e, AL, stride=KK), :] for e in range(2)]
                sbuf[q, i, p * 16 : (p + 1) * 16, :] = jnp.concatenate(pair, axis=0).astype(BF16)
            return 0

        lax.fori_loop(0, NC, turn, 0)
        for d in range(1, NC):
            to = lax.rem(c + d, NC)
            remote(sbuf.at[q, to], abuf.at[q, c], s_ch.at[q, d], r_ch.at[q, d], {"chan": to, "row": r}).start()
        abuf[q, c] = sbuf[q, c]

    row_own = [h * 4 + v for v in (z, zp, z2, zm)]
    row_oth = [(1 - h) * 4 + v for v in (z, zp, z2, zm)]
    h_bw = ym // 2
    h_fw = yp // 2

    def part(row, q, half=None):
        if half is None:
            return g.at[row, pl.ds(q * CH, CH)]
        return g.at[row, pl.ds(q * CH + half * HALF, HALF)]

    sent = []

    def send(q, kind, src, dst, dev):
        cp = remote(src, dst, s_g.at[q, kind], r_g.at[q, kind], dev)
        cp.start()
        sent.append(cp)

    def arrived(q, kind, dst, dev):
        remote(dst, dst, s_g.at[q, kind], r_g.at[q, kind], dev).wait_recv()

    def phase0(q):
        for d in range(1, NC):
            frm = lax.rem(c + NC - d, NC)
            remote(sbuf.at[q, frm], abuf.at[q, frm], s_ch.at[q, d], r_ch.at[q, d], {"chan": frm, "row": r}).wait_recv()
        fl = flags[pl.ds(pl.multiple_of(r * ROWS, ROWS), ROWS), :]
        for p in range(CH // 2):
            x = abuf[q, :, p * 16 : (p + 1) * 16, :].astype(F32)
            for e in range(2):
                v = x[:, e * AL : (e + 1) * AL, :].reshape(ROWS, 128) * fl
                g[r, q * CH + 2 * p + e] = v.astype(BF16)
        send(q, 0, part(r, q), part(r, q), up)
        send(q, 1, part(r, q), part(r, q), dn)
        send(q, 4, part(r, q, 0), transit.at[0, q], fw)
        send(q, 5, part(r, q, 1), transit.at[1, q], bw)

    def phase1(q):
        arrived(q, 0, part(row_own[3], q), dn)
        send(q, 2, part(row_own[3], q, 0), part(row_own[3], q, 0), up)
        arrived(q, 1, part(row_own[1], q), up)
        send(q, 3, part(row_own[1], q, 1), part(row_own[1], q, 1), dn)
        arrived(q, 4, transit.at[0, q], bw)
        send(q, 6, transit.at[0, q], part(h_bw * 4 + z, q, 0), fw)
        arrived(q, 5, transit.at[1, q], fw)
        send(q, 7, transit.at[1, q], part(h_fw * 4 + z, q, 1), bw)

    def phase2(q):
        arrived(q, 6, part(row_oth[0], q, 0), bw)
        send(q, 8, part(row_oth[0], q, 0), part(row_oth[0], q, 0), up)
        send(q, 10, part(row_oth[0], q, 0), part(row_oth[0], q, 0), dn)
        arrived(q, 7, part(row_oth[0], q, 1), fw)
        send(q, 9, part(row_oth[0], q, 1), part(row_oth[0], q, 1), up)
        send(q, 11, part(row_oth[0], q, 1), part(row_oth[0], q, 1), dn)
        arrived(q, 2, part(row_own[2], q, 0), dn)
        send(q, 12, part(row_own[2], q, 0), transit.at[2, q], fw)
        arrived(q, 3, part(row_own[2], q, 1), up)
        send(q, 13, part(row_own[2], q, 1), transit.at[3, q], bw)

    def phase3(q):
        arrived(q, 12, transit.at[2, q], bw)
        send(q, 14, transit.at[2, q], part(h_bw * 4 + z2, q, 0), fw)
        arrived(q, 13, transit.at[3, q], fw)
        send(q, 15, transit.at[3, q], part(h_fw * 4 + z2, q, 1), bw)

    lane = lax.broadcasted_iota(jnp.int32, (32, 128), 1) < 64
    outs = []

    def phase4(q):
        arrived(q, 8, part(row_oth[3], q, 0), dn)
        arrived(q, 9, part(row_oth[3], q, 1), dn)
        arrived(q, 10, part(row_oth[1], q, 0), up)
        arrived(q, 11, part(row_oth[1], q, 1), up)
        arrived(q, 14, part(row_oth[2], q, 0), bw)
        arrived(q, 15, part(row_oth[2], q, 1), fw)
        cp = pltpu.make_async_copy(
            g.at[:, pl.ds(q * CH, CH)], g_out.at[:, pl.ds(q * CH, CH)], s_out.at[q]
        )
        cp.start()
        outs.append(cp)

        def beams(i, _):
            ch = q * CH + i
            x = g[:, ch].reshape(A, 128)
            acc = jnp.dot(wall[ch], x, preferred_element_type=F32)
            turned = pltpu.roll(acc[32:, :], 64, 1)
            bs[pl.ds(pl.multiple_of(ch * 32, 32), 32), :] = acc[:32, :] + jnp.where(lane, -turned, turned)
            return 0

        lax.fori_loop(0, CH, beams, 0)

    for s in range(Q + 4):
        for k, phase in enumerate((phase0, phase1, phase2, phase3, phase4)):
            if 0 <= s - k < Q:
                phase(s - k)

    def pack(i, _):
        for e in range(2):
            bsend[i, e] = bs[pl.ds(e * 16 + i, CHB, stride=32), :].astype(BF16)
        return 0

    lax.fori_loop(0, NC, pack, 0)
    beam_sends = []
    for d in range(1, NC):
        to = lax.rem(c + d, NC)
        cp = remote(bsend.at[to], z_in.at[c], s_bm.at[d], r_bm.at[d], {"chan": to, "row": r})
        cp.start()
        beam_sends.append(cp)
    z_in[c] = bsend[c]
    for d in range(1, NC):
        frm = lax.rem(c + NC - d, NC)
        remote(bsend.at[frm], z_in.at[frm], s_bm.at[d], r_bm.at[d], {"chan": frm, "row": r}).wait_recv()
    for e in range(2):
        zt = z_in[:, e].reshape(NCH, 128).astype(F32).T.astype(BF16)
        series[e] = jnp.dot(zt[:F, :], ptab[...], preferred_element_type=F32) + jnp.dot(
            zt[F:, :], qtab[...], preferred_element_type=F32
        )

    for cp in row_sends:
        cp.wait_send()
    for q in range(Q):
        for d in range(1, NC):
            to = lax.rem(c + d, NC)
            remote(sbuf.at[q, to], abuf.at[q, c], s_ch.at[q, d], r_ch.at[q, d], {"chan": to, "row": r}).wait_send()
    for cp in sent:
        cp.wait_send()
    for cp in beam_sends:
        cp.wait_send()
    for cp in outs:
        cp.wait()


def front(samples, history, taps, flags, delays):
    vmem = pl.BlockSpec(memory_space=pltpu.VMEM)
    hbm = pl.BlockSpec(memory_space=pl.ANY)
    dma = pltpu.SemaphoreType.DMA
    return pl.pallas_call(
        front_kernel,
        out_shape=(
            jax.ShapeDtypeStruct((NR, CHB, ROWS, 128), BF16),
            jax.ShapeDtypeStruct((2, F, FL), F32),
        ),
        in_specs=[vmem, hbm, vmem, vmem, vmem],
        out_specs=(hbm, vmem),
        scratch_shapes=[
            pltpu.VMEM((AL, HIST + F * FL), BF16),
            pltpu.VMEM((F * AL, 128), F32),
            pltpu.VMEM((F * AL, FL), BF16),
            pltpu.VMEM((NCH, FL), BF16),
            pltpu.VMEM((NCH, FL), BF16),
            pltpu.VMEM((AL * KK, 128), F32),
            pltpu.VMEM((Q, NC, CH * AL, 128), BF16),
            pltpu.VMEM((Q, NC, CH * AL, 128), BF16),
            pltpu.VMEM((NR, CHB, ROWS, 128), BF16),
            pltpu.VMEM((4, Q, HALF, ROWS, 128), BF16),
            pltpu.VMEM((32, A), jnp.int32),
            pltpu.VMEM((CHB, 64, A), BF16),
            pltpu.VMEM((CHB * 32, 128), F32),
            pltpu.VMEM((NC, 2, CHB, 128), BF16),
            pltpu.VMEM((NC, 2, CHB, 128), BF16),
            pltpu.VMEM((NCH, FL), BF16),
            pltpu.VMEM((NCH, FL), BF16),
            dma((NR,)),
            dma((NR,)),
            dma((2,)),
            dma((Q, NC)),
            dma((Q, NC)),
            dma((Q, NKIND)),
            dma((Q, NKIND)),
            dma((NC,)),
            dma((NC,)),
            dma((Q,)),
        ],
        compiler_params=pltpu.CompilerParams(
            collective_id=0, has_side_effects=True, vmem_limit_bytes=58 * 2**20
        ),
        name="front",
    )(samples, history, taps, flags, delays)


CB = 2


def gram_kernel(g, out):
    r = lax.axis_index("row")
    low = lax.broadcasted_iota(jnp.int32, (ROWS, 128), 1) < 64
    for i in range(CB):
        own = g[r, i]
        turned = pltpu.roll(own.astype(F32), 64, 1)
        lhs = jnp.concatenate([own, jnp.where(low, turned, -turned).astype(BF16)], axis=0)
        acc = nt(lhs, g[:, i].reshape(A, 128)) * (1.0 / F)
        out[i, 0] = acc[:ROWS].astype(BF16)
        out[i, 1] = acc[ROWS:].astype(BF16)


def gram(g):
    return pl.pallas_call(
        gram_kernel,
        out_shape=jax.ShapeDtypeStruct((CHB, 2, ROWS, A), BF16),
        grid=(CHB // CB,),
        in_specs=[pl.BlockSpec((NR, CB, ROWS, 128), lambda i: (0, i, 0, 0))],
        out_specs=pl.BlockSpec((CB, 2, ROWS, A), lambda i: (i, 0, 0, 0)),
        name="gram",
    )(g)


def body(samples, history, antenna_flags, beam_delays):
    flags = jnp.broadcast_to(antenna_flags.astype(F32)[:, None], (A, 128))
    g, series = front(samples, history, jnp.asarray(tap_table()), flags, beam_delays)
    return gram(g), series


def solution(mesh):
    in_specs = (P(None, "chan", "row"), P(None, "chan", None), P(), P())
    out_specs = (P("chan", None, "row", None), P(("chan", "row"), None, None))
    return jax.shard_map(body, mesh=mesh, in_specs=in_specs, out_specs=out_specs, check_vma=False)
```

```python
import math

import jax
import jax.numpy as jnp
import numpy as np
from jax import lax
from jax.experimental import pallas as pl
from jax.experimental.pallas import tpu as pltpu
from jax.sharding import PartitionSpec as P

A = 1024
FL = 1024
NCH = 512
TAPS = 8
BEAMS = 256
NC = 16
NR = 8
CHB = NCH // NC
ROWS = A // NR
AL = ROWS // NC
F = 64
Q = 4
CH = CHB // Q
KK = NC * CH
HALF = CH // 2
HIST = (TAPS - 1) * FL
SPAN = (F // NR) * FL
MESH = pl.DeviceIdType.MESH
F32 = jnp.float32
BF16 = jnp.bfloat16
NKIND = 16


def tap_table():
    position = (np.arange(TAPS * FL, dtype=np.int32).astype(np.float32) + np.float32(0.5)).astype(np.float64)
    centred = position / FL - TAPS / 2.0
    window = 0.5 - 0.5 * np.cos(2.0 * math.pi * position / (TAPS * FL))
    return (np.sinc(centred) * window).reshape(TAPS, FL).astype(np.float32)


def cos_sin(m):
    quarter = lax.shift_right_logical(m, 8)
    x = ((m & 255) - 128).astype(F32) * (2.0 * math.pi / FL)
    x2 = x * x
    s = x * (1.0 + x2 * (-1.0 / 6 + x2 * (1.0 / 120 + x2 * (-1.0 / 5040 + x2 * (1.0 / 362880)))))
    c = 1.0 + x2 * (-0.5 + x2 * (1.0 / 24 + x2 * (-1.0 / 720 + x2 * (1.0 / 40320 + x2 * (-1.0 / 3628800)))))
    root = math.sqrt(0.5)
    ca = (c - s) * root
    sa = (c + s) * root
    odd = (quarter & 1) == 1
    neg = quarter >= 2
    cv = jnp.where(odd, -sa, ca)
    sv = jnp.where(odd, ca, sa)
    return jnp.where(neg, -cv, cv), jnp.where(neg, -sv, sv)


def nt(lhs, rhs):
    return lax.dot_general(lhs, rhs, (((1,), (1,)), ((), ())), preferred_element_type=F32)


def gram_lhs(own):
    low = lax.broadcasted_iota(jnp.int32, (ROWS, 128), 1) < 64
    turned = pltpu.roll(own.astype(F32), 64, 1)
    return jnp.concatenate([own, jnp.where(low, turned, -turned).astype(BF16)], axis=0) * BF16(1.0 / F)


def front_kernel(
    samples, history, taps, flags, delays, g, vis, z_in, ptab, qtab,
    ext, hop, filt32, filt, dftc, dfts, tmp, sbuf, abuf, transit, fl, wcos, wall, bs, bsend,
    s_row, r_row, s_hop, r_hop, s_far, r_far, s_loc, s_ch, r_ch, s_g, r_g, s_bm, r_bm,
):
    c = lax.axis_index("chan")
    r = lax.axis_index("row")
    c_low = lax.rem(c, 8)
    y_lo = c // 8
    h = r // 4
    z = lax.rem(r, 4)
    y = 2 * h + y_lo
    zp = lax.rem(z + 1, 4)
    zm = lax.rem(z + 3, 4)
    z2 = lax.rem(z + 2, 4)
    yp = lax.rem(y + 1, 4)
    ym = lax.rem(y + 3, 4)
    h_fw = yp // 2
    h_bw = ym // 2
    c_fw = lax.rem(yp, 2) * 8 + c_low
    c_bw = lax.rem(ym, 2) * 8 + c_low
    up = {"chan": c, "row": h * 4 + zp}
    dn = {"chan": c, "row": h * 4 + zm}
    fw = {"chan": c_fw, "row": h_fw * 4 + z}
    bw = {"chan": c_bw, "row": h_bw * 4 + z}
    fw_up = {"chan": c_fw, "row": h_fw * 4 + zp}
    bw_dn = {"chan": c_bw, "row": h_bw * 4 + zm}
    row_own = [h * 4 + v for v in (z, zp, z2, zm)]
    row_oth = [(1 - h) * 4 + v for v in (z, zp, z2, zm)]

    def remote(src, dst, ss, rs, dev):
        return pltpu.make_async_remote_copy(
            src_ref=src, dst_ref=dst, send_sem=ss, recv_sem=rs, device_id=dev, device_id_type=MESH
        )

    barrier = pltpu.get_barrier_semaphore()
    for d in range(1, NR):
        pl.semaphore_signal(barrier, inc=1, device_id={"chan": c, "row": lax.rem(r + d, NR)}, device_id_type=MESH)
    for d in range(1, NC):
        pl.semaphore_signal(barrier, inc=1, device_id={"chan": lax.rem(c + d, NC), "row": r}, device_id_type=MESH)
    for dev in (fw, bw, fw_up, bw_dn):
        pl.semaphore_signal(barrier, inc=1, device_id=dev, device_id_type=MESH)
    pl.semaphore_wait(barrier, NR - 1 + NC - 1 + 4)

    def span(row):
        return ext.at[:, pl.ds(pl.multiple_of(HIST + row * SPAN, FL), SPAN)]

    copies = []

    def start(cp):
        cp.start()
        copies.append(cp)

    start(remote(samples.at[row_oth[0]], hop.at[0], s_hop.at[0], r_hop.at[0], fw))
    start(remote(samples.at[row_oth[3]], hop.at[2], s_hop.at[2], r_hop.at[2], bw))
    start(remote(samples.at[row_oth[2]], hop.at[3], s_hop.at[3], r_hop.at[3], bw_dn))
    start(remote(samples.at[row_oth[1]], hop.at[1], s_hop.at[1], r_hop.at[1], fw))
    for d in (2, 1, 3):
        to = row_own[d]
        start(remote(samples.at[to], span(r), s_row.at[d], r_row.at[d], {"chan": c, "row": to}))
    own = pltpu.make_async_copy(samples.at[r], span(r), s_loc.at[0])
    own.start()
    hist = pltpu.make_async_copy(history.at[r], ext.at[:, pl.ds(0, HIST)], s_loc.at[1])
    hist.start()

    def dft_rows(i, _):
        row = i * 16 + lax.broadcasted_iota(jnp.int32, (16, FL), 0)
        q, rest = row // KK, row % KK
        k = (rest // CH) * CHB + q * CH + rest % CH
        n = lax.broadcasted_iota(jnp.int32, (16, FL), 1)
        cv, sv = cos_sin((k * n) & (FL - 1))
        scale = 1.0 / math.sqrt(FL)
        at = pl.ds(pl.multiple_of(i * 16, 16), 16)
        dftc[at, :] = (cv * scale).astype(BF16)
        dfts[at, :] = (-sv * scale).astype(BF16)
        return 0

    lax.fori_loop(0, NCH // 16, dft_rows, 0)

    for k, frm, origin, dev in (
        (0, bw, h_bw * 4 + z, fw),
        (2, fw, h_fw * 4 + z, bw_dn),
        (3, fw_up, h_fw * 4 + zp, bw_dn),
        (1, bw, h_bw * 4 + z, fw_up),
    ):
        remote(hop.at[k], hop.at[k], s_hop.at[k], r_hop.at[k], frm).wait_recv()
        start(remote(hop.at[k], span(origin), s_far.at[k], r_far.at[k], dev))

    def synth_rows(i, _):
        k = i * 16 + lax.broadcasted_iota(jnp.int32, (16, FL), 0)
        n = lax.broadcasted_iota(jnp.int32, (16, FL), 1)
        cv, sv = cos_sin((k * n) & (FL - 1))
        scale = 1.0 / math.sqrt(NCH)
        at = pl.ds(pl.multiple_of(i * 16, 16), 16)
        ptab[at, :] = (cv * scale).astype(BF16)
        qtab[at, :] = (-sv * scale).astype(BF16)
        return 0

    lax.fori_loop(0, NCH // 16, synth_rows, 0)

    for e in range(2):
        for i in range(NC):
            wcos[e * NC + i : e * NC + i + 1, :] = delays[pl.ds(i * 2 * NR + 2 * r + e, 1), :]

    def steer(i, _):
        lanes = pl.ds(pl.multiple_of(i * 128, 128), 128)
        d = wcos[:, lanes]
        cr, ci = cos_sin((d * (c * CHB)) & (FL - 1))
        sr, si = cos_sin(d)
        scale = 1.0 / math.sqrt(A)
        for ch in range(CHB):
            wall[ch, 0:32, lanes] = (cr * scale).astype(BF16)
            wall[ch, 32:64, lanes] = (-ci * scale).astype(BF16)
            cr, ci = cr * sr - ci * si, cr * si + ci * sr
        return 0

    lax.fori_loop(0, A // 128, steer, 0)
    fl[...] = jnp.broadcast_to(flags[pl.ds(r, 1), :].astype(F32), (ROWS, 128)).T

    own.wait()
    hist.wait()
    for d, frm in ((1, row_own[3]), (2, row_own[2]), (3, row_own[1])):
        remote(samples.at[frm], span(frm), s_row.at[d], r_row.at[d], {"chan": c, "row": frm}).wait_recv()
    for k, origin in ((0, row_oth[0]), (1, row_oth[3]), (2, row_oth[1]), (3, row_oth[2])):
        remote(hop.at[k], span(origin), s_far.at[k], r_far.at[k], fw).wait_recv()

    def pfb(i, _):
        lanes = pl.ds(pl.multiple_of(i * 128, 128), 128)
        tap = [jnp.broadcast_to(taps[t : t + 1, lanes], (AL, 128)) for t in range(TAPS)]
        win = [ext[:, pl.ds(pl.multiple_of(t * FL + i * 128, 128), 128)].astype(F32) for t in range(TAPS - 1)]
        for f in range(F):
            win.append(ext[:, pl.ds(pl.multiple_of((f + TAPS - 1) * FL + i * 128, 128), 128)].astype(F32))
            acc = win[f] * tap[0]
            for t in range(1, TAPS):
                acc = acc + win[f + t] * tap[t]
            filt32[f * AL : (f + 1) * AL, :] = acc
        for a in range(AL):
            for b in range(F // 16):
                filt[a * F + b * 16 : a * F + (b + 1) * 16, lanes] = filt32[
                    pl.ds(b * 16 * AL + a, 16, stride=AL), :
                ].astype(BF16)
        return 0

    lax.fori_loop(0, FL // 128, pfb, 0)

    low = lax.broadcasted_iota(jnp.int32, (KK, 128), 1) < 64

    def spectra(q):
        rows = slice(q * KK, (q + 1) * KK)
        re = nt(dftc[rows, :], filt[...])
        im = nt(dfts[rows, :], filt[...])
        for t in range(AL // 2):
            rt = re[:, t * 128 : (t + 1) * 128]
            it = im[:, t * 128 : (t + 1) * 128]
            tmp[(2 * t) * KK : (2 * t + 1) * KK, :] = jnp.where(low, rt, pltpu.roll(it, 64, 1))
            tmp[(2 * t + 1) * KK : (2 * t + 2) * KK, :] = jnp.where(low, pltpu.roll(rt, 64, 1), it)

        def turn(i, _):
            for p in range(CH // 2):
                pair = [tmp[pl.ds(i * CH + 2 * p + e, AL, stride=KK), :] for e in range(2)]
                sbuf[q, i, p * 16 : (p + 1) * 16, :] = jnp.concatenate(pair, axis=0).astype(BF16)
            return 0

        lax.fori_loop(0, NC, turn, 0)
        for d in range(1, NC):
            to = lax.rem(c + d, NC)
            start(remote(sbuf.at[q, to], abuf.at[q, c], s_ch.at[q, d], r_ch.at[q, d], {"chan": to, "row": r}))
        abuf[q, c] = sbuf[q, c]

    def part(row, q, half=None):
        if half is None:
            return g.at[row, pl.ds(q * CH, CH)]
        return g.at[row, pl.ds(q * CH + half * HALF, HALF)]

    def send(q, kind, src, dst, dev):
        start(remote(src, dst, s_g.at[q, kind], r_g.at[q, kind], dev))

    def arrived(q, kind, dst, dev):
        remote(dst, dst, s_g.at[q, kind], r_g.at[q, kind], dev).wait_recv()

    def own_block(q):
        for d in range(1, NC):
            frm = lax.rem(c + NC - d, NC)
            remote(sbuf.at[q, frm], abuf.at[q, frm], s_ch.at[q, d], r_ch.at[q, d], {"chan": frm, "row": r}).wait_recv()
        for p in range(CH // 2):
            x = abuf[q, :, p * 16 : (p + 1) * 16, :].astype(F32)
            for e in range(2):
                v = x[:, e * AL : (e + 1) * AL, :].reshape(ROWS, 128) * fl[...]
                g[r, q * CH + 2 * p + e] = v.astype(BF16)
        send(q, 4, part(r, q, 0), transit.at[0, q], fw)
        send(q, 5, part(r, q, 1), transit.at[1, q], bw)
        send(q, 0, part(r, q), part(r, q), up)
        send(q, 1, part(r, q), part(r, q), dn)

    def cross(q):
        arrived(q, 4, transit.at[0, q], bw)
        send(q, 6, transit.at[0, q], part(h_bw * 4 + z, q, 0), fw)
        arrived(q, 5, transit.at[1, q], fw)
        send(q, 7, transit.at[1, q], part(h_fw * 4 + z, q, 1), bw)

    def relay(q):
        arrived(q, 0, part(row_own[3], q), dn)
        send(q, 2, part(row_own[3], q, 0), part(row_own[3], q, 0), up)
        arrived(q, 1, part(row_own[1], q), up)
        send(q, 3, part(row_own[1], q, 1), part(row_own[1], q, 1), dn)

    def spread(q):
        arrived(q, 6, part(row_oth[0], q, 0), bw)
        send(q, 8, part(row_oth[0], q, 0), part(row_oth[0], q, 0), up)
        send(q, 10, part(row_oth[0], q, 0), part(row_oth[0], q, 0), dn)
        arrived(q, 7, part(row_oth[0], q, 1), fw)
        send(q, 9, part(row_oth[0], q, 1), part(row_oth[0], q, 1), up)
        send(q, 11, part(row_oth[0], q, 1), part(row_oth[0], q, 1), dn)

    def cross2(q):
        arrived(q, 2, part(row_own[2], q, 0), dn)
        send(q, 12, part(row_own[2], q, 0), transit.at[2, q], fw)
        arrived(q, 3, part(row_own[2], q, 1), up)
        send(q, 13, part(row_own[2], q, 1), transit.at[3, q], bw)

    def cross3(q):
        arrived(q, 12, transit.at[2, q], bw)
        send(q, 14, transit.at[2, q], part(h_bw * 4 + z2, q, 0), fw)
        arrived(q, 13, transit.at[3, q], fw)
        send(q, 15, transit.at[3, q], part(h_fw * 4 + z2, q, 1), bw)

    lane = lax.broadcasted_iota(jnp.int32, (32, 128), 1) < 64

    def use(q):
        arrived(q, 8, part(row_oth[3], q, 0), dn)
        arrived(q, 9, part(row_oth[3], q, 1), dn)
        arrived(q, 10, part(row_oth[1], q, 0), up)
        arrived(q, 11, part(row_oth[1], q, 1), up)
        arrived(q, 14, part(row_oth[2], q, 0), bw)
        arrived(q, 15, part(row_oth[2], q, 1), fw)

        def beams(i, _):
            ch = q * CH + i
            acc = jnp.dot(wall[ch], g[:, ch].reshape(A, 128), preferred_element_type=F32)
            turned = pltpu.roll(acc[32:, :], 64, 1)
            bs[pl.ds(pl.multiple_of(i * 32, 32), 32), :] = acc[:32, :] + jnp.where(lane, -turned, turned)
            return 0

        lax.fori_loop(0, CH, beams, 0)

        def pack(i, _):
            pair = [bs[pl.ds(e * 16 + i, CH, stride=32), :] for e in range(2)]
            bsend[q, i] = jnp.concatenate(pair, axis=0).astype(BF16)
            return 0

        lax.fori_loop(0, NC, pack, 0)
        for d in range(1, NC):
            to = lax.rem(c + d, NC)
            start(remote(bsend.at[q, to], z_in.at[q, c], s_bm.at[q, d], r_bm.at[q, d], {"chan": to, "row": r}))
        z_in[q, c] = bsend[q, c]

    def gram_chunk(q):
        def gram(i, _):
            ch = q * CH + i
            acc = nt(gram_lhs(g[r, ch]), g[:, ch].reshape(A, 128))
            vis[ch, 0] = acc[:ROWS].astype(BF16)
            vis[ch, 1] = acc[ROWS:].astype(BF16)
            return 0

        lax.fori_loop(0, CH, gram, 0)

    spectra(0)
    spectra(1)
    spectra(2)
    own_block(0)
    spectra(3)
    own_block(1)
    cross(0)
    own_block(2)
    cross(1)
    relay(0)
    own_block(3)
    cross(2)
    spread(0)
    relay(1)
    cross(3)
    spread(1)
    cross2(0)
    relay(2)
    spread(2)
    cross2(1)
    cross3(0)
    relay(3)
    spread(3)
    cross2(2)
    cross3(1)
    use(0)
    gram_chunk(0)
    cross2(3)
    cross3(2)
    use(1)
    cross3(3)
    gram_chunk(1)
    use(2)
    gram_chunk(2)
    use(3)

    for q in range(Q):
        for d in range(1, NC):
            frm = lax.rem(c + NC - d, NC)
            remote(bsend.at[q, frm], z_in.at[q, frm], s_bm.at[q, d], r_bm.at[q, d], {"chan": frm, "row": r}).wait_recv()
    for cp in copies:
        cp.wait_send()


def front(samples, history, taps, flags, delays):
    vmem = pl.BlockSpec(memory_space=pltpu.VMEM)
    hbm = pl.BlockSpec(memory_space=pl.ANY)
    dma = pltpu.SemaphoreType.DMA
    return pl.pallas_call(
        front_kernel,
        out_shape=(
            pltpu.VMEM((NR, CHB, ROWS, 128), BF16),
            pltpu.VMEM((CHB - CH, 2, ROWS, A), BF16),
            pltpu.VMEM((Q, NC, 2 * CH, 128), BF16),
            pltpu.VMEM((NCH, FL), BF16),
            pltpu.VMEM((NCH, FL), BF16),
        ),
        in_specs=[vmem, hbm, vmem, vmem, vmem],
        out_specs=(vmem,) * 5,
        scratch_shapes=[
            pltpu.VMEM((AL, HIST + F * FL), BF16),
            pltpu.VMEM((4, AL, SPAN), BF16),
            pltpu.VMEM((F * AL, 128), F32),
            pltpu.VMEM((F * AL, FL), BF16),
            pltpu.VMEM((NCH, FL), BF16),
            pltpu.VMEM((NCH, FL), BF16),
            pltpu.VMEM((AL * KK, 128), F32),
            pltpu.VMEM((Q, NC, CH * AL, 128), BF16),
            pltpu.VMEM((Q, NC, CH * AL, 128), BF16),
            pltpu.VMEM((4, Q, HALF, ROWS, 128), BF16),
            pltpu.VMEM((ROWS, 128), F32),
            pltpu.VMEM((32, A), jnp.int32),
            pltpu.VMEM((CHB, 64, A), BF16),
            pltpu.VMEM((CH * 32, 128), F32),
            pltpu.VMEM((Q, NC, 2 * CH, 128), BF16),
            dma((4,)),
            dma((4,)),
            dma((4,)),
            dma((4,)),
            dma((4,)),
            dma((4,)),
            dma((2,)),
            dma((Q, NC)),
            dma((Q, NC)),
            dma((Q, NKIND)),
            dma((Q, NKIND)),
            dma((Q, NC)),
            dma((Q, NC)),
        ],
        compiler_params=pltpu.CompilerParams(
            collective_id=0, has_side_effects=True, vmem_limit_bytes=FRONT_VMEM
        ),
        name="front",
    )(samples, history, taps, flags, delays)


FRONT_VMEM = 40 * 2**20
PARTS = 6


def back_kernel(g, vis, z_in, ptab, qtab, out, series, last, s_vis, s_last):
    r = lax.axis_index("row")
    step = (CHB - CH) // PARTS
    copies = [
        pltpu.make_async_copy(vis.at[pl.ds(i * step, step)], out.at[pl.ds(i * step, step)], s_vis.at[i])
        for i in range(PARTS)
    ]
    for cp in copies:
        cp.start()

    def place(i):
        return pltpu.make_async_copy(last.at[i], out.at[CHB - CH + i], s_last.at[i])

    def gram(i, _):
        ch = CHB - CH + i
        acc = nt(gram_lhs(g[r, ch]), g[:, ch].reshape(A, 128))
        last[i, 0] = acc[:ROWS].astype(BF16)
        last[i, 1] = acc[ROWS:].astype(BF16)
        place(i).start()
        return 0

    lax.fori_loop(0, CH, gram, 0)
    for e in range(2):
        rows = [z_in[q, i].astype(F32)[e * CH : (e + 1) * CH] for i in range(NC) for q in range(Q)]
        zt = jnp.concatenate(rows, axis=0).T.astype(BF16)
        series[e] = jnp.dot(zt[:F, :], ptab[...], preferred_element_type=F32) + jnp.dot(
            zt[F:, :], qtab[...], preferred_element_type=F32
        )
    for cp in copies:
        cp.wait()

    def finish(i, _):
        place(i).wait()
        return 0

    lax.fori_loop(0, CH, finish, 0)


def back(g, vis, z_in, ptab, qtab):
    vmem = pl.BlockSpec(memory_space=pltpu.VMEM)
    return pl.pallas_call(
        back_kernel,
        out_shape=(
            jax.ShapeDtypeStruct((CHB, 2, ROWS, A), BF16),
            jax.ShapeDtypeStruct((2, F, FL), F32),
        ),
        in_specs=[vmem] * 5,
        out_specs=(pl.BlockSpec(memory_space=pl.ANY), vmem),
        scratch_shapes=[
            pltpu.VMEM((CH, 2, ROWS, A), BF16),
            pltpu.SemaphoreType.DMA((PARTS,)),
            pltpu.SemaphoreType.DMA((CH,)),
        ],
        compiler_params=pltpu.CompilerParams(vmem_limit_bytes=BACK_VMEM),
        name="back",
    )(g, vis, z_in, ptab, qtab)


BACK_VMEM = 12 * 2**20


def body(samples, history, antenna_flags, beam_delays):
    held = front(samples, history, jnp.asarray(tap_table()), antenna_flags.reshape(NR, ROWS), beam_delays)
    return back(*held)


def solution(mesh):
    in_specs = (P(None, "chan", "row"), P(None, "chan", None), P(), P())
    out_specs = (P("chan", None, "row", None), P(("chan", "row"), None, None))
    return jax.shard_map(body, mesh=mesh, in_specs=in_specs, out_specs=out_specs, check_vma=False)
```

```python
import math

import jax
import jax.numpy as jnp
import numpy as np
from jax import lax
from jax.experimental import pallas as pl
from jax.experimental.pallas import tpu as pltpu
from jax.sharding import PartitionSpec as P

A = 1024
FL = 1024
NCH = 512
TAPS = 8
BEAMS = 256
NC = 16
NR = 8
CHB = NCH // NC
ROWS = A // NR
AL = ROWS // NC
F = 64
Q = 4
CH = CHB // Q
KK = NC * CH
HALF = CH // 2
HIST = (TAPS - 1) * FL
SPAN = (F // NR) * FL
MESH = pl.DeviceIdType.MESH
F32 = jnp.float32
BF16 = jnp.bfloat16
NKIND = 11


def tap_table():
    position = (np.arange(TAPS * FL, dtype=np.int32).astype(np.float32) + np.float32(0.5)).astype(np.float64)
    centred = position / FL - TAPS / 2.0
    window = 0.5 - 0.5 * np.cos(2.0 * math.pi * position / (TAPS * FL))
    return (np.sinc(centred) * window).reshape(TAPS, FL).astype(np.float32)


def cos_sin(m):
    quarter = lax.shift_right_logical(m, 8)
    x = ((m & 255) - 128).astype(F32) * (2.0 * math.pi / FL)
    x2 = x * x
    s = x * (1.0 + x2 * (-1.0 / 6 + x2 * (1.0 / 120 + x2 * (-1.0 / 5040 + x2 * (1.0 / 362880)))))
    c = 1.0 + x2 * (-0.5 + x2 * (1.0 / 24 + x2 * (-1.0 / 720 + x2 * (1.0 / 40320 + x2 * (-1.0 / 3628800)))))
    root = math.sqrt(0.5)
    ca = (c - s) * root
    sa = (c + s) * root
    odd = (quarter & 1) == 1
    neg = quarter >= 2
    cv = jnp.where(odd, -sa, ca)
    sv = jnp.where(odd, ca, sa)
    return jnp.where(neg, -cv, cv), jnp.where(neg, -sv, sv)


def nt(lhs, rhs):
    return lax.dot_general(lhs, rhs, (((1,), (1,)), ((), ())), preferred_element_type=F32)


def gram_lhs(own):
    low = lax.broadcasted_iota(jnp.int32, (ROWS, 128), 1) < 64
    turned = pltpu.roll(own.astype(F32), 64, 1)
    return jnp.concatenate([own, jnp.where(low, turned, -turned).astype(BF16)], axis=0) * BF16(1.0 / F)


def front_kernel(
    samples, history, taps, flags, delays, g, vis, z_in, ptab, qtab,
    ext, dl, filt32, filt, dftc, dfts, tmp, sbuf, abuf, fl, wcos, wall, bs, bsend,
    s_row, r_row, s_loc, s_ch, r_ch, s_g, r_g, s_bm, r_bm,
):
    c = lax.axis_index("chan")
    r = lax.axis_index("row")
    h = r // 4
    z = lax.rem(r, 4)
    zp = lax.rem(z + 1, 4)
    zm = lax.rem(z + 3, 4)
    z2 = lax.rem(z + 2, 4)
    up = {"chan": c, "row": h * 4 + zp}
    dn = {"chan": c, "row": h * 4 + zm}
    over = {"chan": c, "row": (1 - h) * 4 + z}
    row_own = [h * 4 + v for v in (z, zp, z2, zm)]
    row_oth = [(1 - h) * 4 + v for v in (z, zp, z2, zm)]

    def remote(src, dst, ss, rs, dev):
        return pltpu.make_async_remote_copy(
            src_ref=src, dst_ref=dst, send_sem=ss, recv_sem=rs, device_id=dev, device_id_type=MESH
        )

    barrier = pltpu.get_barrier_semaphore()
    for d in range(1, NR):
        pl.semaphore_signal(barrier, inc=1, device_id={"chan": c, "row": lax.rem(r + d, NR)}, device_id_type=MESH)
    for d in range(1, NC):
        pl.semaphore_signal(barrier, inc=1, device_id={"chan": lax.rem(c + d, NC), "row": r}, device_id_type=MESH)
    pl.semaphore_wait(barrier, NR - 1 + NC - 1)

    def span(row):
        return ext.at[:, pl.ds(pl.multiple_of(HIST + row * SPAN, FL), SPAN)]

    copies = []

    def start(cp):
        cp.start()
        copies.append(cp)

    for d in (6, 7, 5, 2, 4, 1, 3):
        to = (row_own + row_oth)[d]
        start(remote(samples.at[to], span(r), s_row.at[d], r_row.at[d], {"chan": c, "row": to}))
    own = pltpu.make_async_copy(samples.at[r], span(r), s_loc.at[0])
    own.start()
    hist = pltpu.make_async_copy(history.at[r], ext.at[:, pl.ds(0, HIST)], s_loc.at[1])
    hist.start()
    late = pltpu.make_async_copy(delays, dl, s_loc.at[2])
    late.start()

    def dft_rows(i, _):
        row = i * 16 + lax.broadcasted_iota(jnp.int32, (16, FL), 0)
        q, rest = row // KK, row % KK
        k = (rest // CH) * CHB + q * CH + rest % CH
        n = lax.broadcasted_iota(jnp.int32, (16, FL), 1)
        cv, sv = cos_sin((k * n) & (FL - 1))
        scale = 1.0 / math.sqrt(FL)
        at = pl.ds(pl.multiple_of(i * 16, 16), 16)
        dftc[at, :] = (cv * scale).astype(BF16)
        dfts[at, :] = (-sv * scale).astype(BF16)
        return 0

    lax.fori_loop(0, NCH // 16, dft_rows, 0)

    def synth_rows(i, _):
        k = i * 16 + lax.broadcasted_iota(jnp.int32, (16, FL), 0)
        n = lax.broadcasted_iota(jnp.int32, (16, FL), 1)
        cv, sv = cos_sin((k * n) & (FL - 1))
        scale = 1.0 / math.sqrt(NCH)
        at = pl.ds(pl.multiple_of(i * 16, 16), 16)
        ptab[at, :] = (cv * scale).astype(BF16)
        qtab[at, :] = (-sv * scale).astype(BF16)
        return 0

    lax.fori_loop(0, NCH // 16, synth_rows, 0)

    late.wait()
    for e in range(2):
        for i in range(NC):
            wcos[e * NC + i : e * NC + i + 1, :] = dl[pl.ds(i * 2 * NR + 2 * r + e, 1), :]

    def steer(i, _):
        lanes = pl.ds(pl.multiple_of(i * 128, 128), 128)
        d = wcos[:, lanes]
        cr, ci = cos_sin((d * (c * CHB)) & (FL - 1))
        sr, si = cos_sin(d)
        scale = 1.0 / math.sqrt(A)
        for ch in range(CHB):
            wall[ch, 0:32, lanes] = (cr * scale).astype(BF16)
            wall[ch, 32:64, lanes] = (-ci * scale).astype(BF16)
            cr, ci = cr * sr - ci * si, cr * si + ci * sr
        return 0

    lax.fori_loop(0, A // 128, steer, 0)
    fl[...] = jnp.broadcast_to(flags[pl.ds(r, 1), :].astype(F32), (ROWS, 128)).T

    own.wait()
    hist.wait()
    for d, frm in (
        (1, row_own[3]), (3, row_own[1]), (2, row_own[2]),
        (4, row_oth[0]), (5, row_oth[3]), (7, row_oth[1]), (6, row_oth[2]),
    ):
        remote(samples.at[frm], span(frm), s_row.at[d], r_row.at[d], {"chan": c, "row": frm}).wait_recv()

    def pfb(i, _):
        lanes = pl.ds(pl.multiple_of(i * 128, 128), 128)
        tap = [jnp.broadcast_to(taps[t : t + 1, lanes], (AL, 128)) for t in range(TAPS)]
        win = [ext[:, pl.ds(pl.multiple_of(t * FL + i * 128, 128), 128)].astype(F32) for t in range(TAPS - 1)]
        for f in range(F):
            win.append(ext[:, pl.ds(pl.multiple_of((f + TAPS - 1) * FL + i * 128, 128), 128)].astype(F32))
            acc = win[f] * tap[0]
            for t in range(1, TAPS):
                acc = acc + win[f + t] * tap[t]
            filt32[f * AL : (f + 1) * AL, :] = acc
        for a in range(AL):
            for b in range(F // 16):
                filt[a * F + b * 16 : a * F + (b + 1) * 16, lanes] = filt32[
                    pl.ds(b * 16 * AL + a, 16, stride=AL), :
                ].astype(BF16)
        return 0

    lax.fori_loop(0, FL // 128, pfb, 0)

    low = lax.broadcasted_iota(jnp.int32, (KK, 128), 1) < 64

    def spectra(q):
        rows = slice(q * KK, (q + 1) * KK)
        re = nt(dftc[rows, :], filt[...])
        im = nt(dfts[rows, :], filt[...])
        for t in range(AL // 2):
            rt = re[:, t * 128 : (t + 1) * 128]
            it = im[:, t * 128 : (t + 1) * 128]
            tmp[(2 * t) * KK : (2 * t + 1) * KK, :] = jnp.where(low, rt, pltpu.roll(it, 64, 1))
            tmp[(2 * t + 1) * KK : (2 * t + 2) * KK, :] = jnp.where(low, pltpu.roll(rt, 64, 1), it)

        def turn(i, _):
            for p in range(CH // 2):
                pair = [tmp[pl.ds(i * CH + 2 * p + e, AL, stride=KK), :] for e in range(2)]
                sbuf[q, i, p * 16 : (p + 1) * 16, :] = jnp.concatenate(pair, axis=0).astype(BF16)
            return 0

        lax.fori_loop(0, NC, turn, 0)
        for d in range(1, NC):
            to = lax.rem(c + d, NC)
            start(remote(sbuf.at[q, to], abuf.at[q, c], s_ch.at[q, d], r_ch.at[q, d], {"chan": to, "row": r}))
        abuf[q, c] = sbuf[q, c]

    def part(row, q, half=None):
        if half is None:
            return g.at[row, pl.ds(q * CH, CH)]
        return g.at[row, pl.ds(q * CH + half * HALF, HALF)]

    def send(q, kind, src, dst, dev):
        start(remote(src, dst, s_g.at[q, kind], r_g.at[q, kind], dev))

    def arrived(q, kind, dst, dev):
        remote(dst, dst, s_g.at[q, kind], r_g.at[q, kind], dev).wait_recv()

    def own_block(q):
        for d in range(1, NC):
            frm = lax.rem(c + NC - d, NC)
            remote(sbuf.at[q, frm], abuf.at[q, frm], s_ch.at[q, d], r_ch.at[q, d], {"chan": frm, "row": r}).wait_recv()
        for p in range(CH // 2):
            x = abuf[q, :, p * 16 : (p + 1) * 16, :].astype(F32)
            for e in range(2):
                v = x[:, e * AL : (e + 1) * AL, :].reshape(ROWS, 128) * fl[...]
                g[r, q * CH + 2 * p + e] = v.astype(BF16)
        send(q, 4, part(r, q), part(r, q), over)
        send(q, 0, part(r, q), part(r, q), up)
        send(q, 1, part(r, q), part(r, q), dn)

    def relay(q):
        arrived(q, 0, part(row_own[3], q), dn)
        send(q, 2, part(row_own[3], q, 0), part(row_own[3], q, 0), up)
        arrived(q, 1, part(row_own[1], q), up)
        send(q, 3, part(row_own[1], q, 1), part(row_own[1], q, 1), dn)

    def relay_tail():
        q = Q - 1
        send(q, 9, part(row_own[3], q, 1), part(row_own[3], q, 1), over)
        send(q, 10, part(row_own[1], q, 1), part(row_own[1], q, 1), over)

    def spread(q):
        half = 0 if q == Q - 1 else None
        arrived(q, 4, part(row_oth[0], q), over)
        send(q, 5, part(row_oth[0], q, half), part(row_oth[0], q, half), up)
        send(q, 6, part(row_oth[0], q, half), part(row_oth[0], q, half), dn)

    def cross(q):
        arrived(q, 2, part(row_own[2], q, 0), dn)
        send(q, 7, part(row_own[2], q, 0), part(row_own[2], q, 0), over)
        arrived(q, 3, part(row_own[2], q, 1), up)
        send(q, 8, part(row_own[2], q, 1), part(row_own[2], q, 1), over)

    lane = lax.broadcasted_iota(jnp.int32, (32, 128), 1) < 64

    def use(q):
        half = 0 if q == Q - 1 else None
        arrived(q, 7, part(row_oth[2], q, 0), over)
        arrived(q, 8, part(row_oth[2], q, 1), over)
        if q == Q - 1:
            arrived(q, 9, part(row_oth[3], q, 1), over)
            arrived(q, 10, part(row_oth[1], q, 1), over)
        arrived(q, 5, part(row_oth[3], q, half), dn)
        arrived(q, 6, part(row_oth[1], q, half), up)

        def beams(i, _):
            ch = q * CH + i
            acc = jnp.dot(wall[ch], g[:, ch].reshape(A, 128), preferred_element_type=F32)
            turned = pltpu.roll(acc[32:, :], 64, 1)
            bs[pl.ds(pl.multiple_of(i * 32, 32), 32), :] = acc[:32, :] + jnp.where(lane, -turned, turned)
            return 0

        lax.fori_loop(0, CH, beams, 0)

        def pack(i, _):
            pair = [bs[pl.ds(e * 16 + i, CH, stride=32), :] for e in range(2)]
            bsend[q, i] = jnp.concatenate(pair, axis=0).astype(BF16)
            return 0

        lax.fori_loop(0, NC, pack, 0)
        for d in range(1, NC):
            to = lax.rem(c + d, NC)
            start(remote(bsend.at[q, to], z_in.at[q, c], s_bm.at[q, d], r_bm.at[q, d], {"chan": to, "row": r}))
        z_in[q, c] = bsend[q, c]

    def gram_chunk(q):
        def gram(i, _):
            ch = q * CH + i
            acc = nt(gram_lhs(g[r, ch]), g[:, ch].reshape(A, 128))
            vis[ch, 0] = acc[:ROWS].astype(BF16)
            vis[ch, 1] = acc[ROWS:].astype(BF16)
            return 0

        lax.fori_loop(0, CH, gram, 0)

    spectra(0)
    spectra(1)
    spectra(2)
    own_block(0)
    spectra(3)
    for q in range(1, Q):
        own_block(q)
    for q in range(Q):
        relay(q)
    relay_tail()
    for q in range(Q):
        spread(q)
    for q in range(Q):
        cross(q)
    for q in range(Q):
        use(q)
        if q < Q - 1:
            gram_chunk(q)

    for q in range(Q):
        for d in range(1, NC):
            frm = lax.rem(c + NC - d, NC)
            remote(bsend.at[q, frm], z_in.at[q, frm], s_bm.at[q, d], r_bm.at[q, d], {"chan": frm, "row": r}).wait_recv()
    for cp in copies:
        cp.wait_send()


def front(samples, history, taps, flags, delays):
    vmem = pl.BlockSpec(memory_space=pltpu.VMEM)
    hbm = pl.BlockSpec(memory_space=pl.ANY)
    dma = pltpu.SemaphoreType.DMA
    return pl.pallas_call(
        front_kernel,
        out_shape=(
            pltpu.VMEM((NR, CHB, ROWS, 128), BF16),
            pltpu.VMEM((CHB - CH, 2, ROWS, A), BF16),
            pltpu.VMEM((Q, NC, 2 * CH, 128), BF16),
            pltpu.VMEM((NCH, FL), BF16),
            pltpu.VMEM((NCH, FL), BF16),
        ),
        in_specs=[hbm, hbm, vmem, vmem, hbm],
        out_specs=(vmem,) * 5,
        scratch_shapes=[
            pltpu.VMEM((AL, HIST + F * FL), BF16),
            pltpu.VMEM((BEAMS, A), jnp.int32),
            pltpu.VMEM((F * AL, 128), F32),
            pltpu.VMEM((F * AL, FL), BF16),
            pltpu.VMEM((NCH, FL), BF16),
            pltpu.VMEM((NCH, FL), BF16),
            pltpu.VMEM((AL * KK, 128), F32),
            pltpu.VMEM((Q, NC, CH * AL, 128), BF16),
            pltpu.VMEM((Q, NC, CH * AL, 128), BF16),
            pltpu.VMEM((ROWS, 128), F32),
            pltpu.VMEM((32, A), jnp.int32),
            pltpu.VMEM((CHB, 64, A), BF16),
            pltpu.VMEM((CH * 32, 128), F32),
            pltpu.VMEM((Q, NC, 2 * CH, 128), BF16),
            dma((NR,)),
            dma((NR,)),
            dma((3,)),
            dma((Q, NC)),
            dma((Q, NC)),
            dma((Q, NKIND)),
            dma((Q, NKIND)),
            dma((Q, NC)),
            dma((Q, NC)),
        ],
        compiler_params=pltpu.CompilerParams(
            collective_id=0, has_side_effects=True, vmem_limit_bytes=FRONT_VMEM
        ),
        name="front",
    )(samples, history, taps, flags, delays)


FRONT_VMEM = 40 * 2**20
PARTS = 6


def back_kernel(g, vis, z_in, ptab, qtab, out, series, last, s_vis, s_last):
    r = lax.axis_index("row")
    step = (CHB - CH) // PARTS
    copies = [
        pltpu.make_async_copy(vis.at[pl.ds(i * step, step)], out.at[pl.ds(i * step, step)], s_vis.at[i])
        for i in range(PARTS)
    ]
    for cp in copies:
        cp.start()

    def place(i):
        return pltpu.make_async_copy(last.at[i], out.at[CHB - CH + i], s_last.at[i])

    def gram(i, _):
        ch = CHB - CH + i
        acc = nt(gram_lhs(g[r, ch]), g[:, ch].reshape(A, 128))
        last[i, 0] = acc[:ROWS].astype(BF16)
        last[i, 1] = acc[ROWS:].astype(BF16)
        place(i).start()
        return 0

    lax.fori_loop(0, CH, gram, 0)
    for e in range(2):
        rows = [z_in[q, i].astype(F32)[e * CH : (e + 1) * CH] for i in range(NC) for q in range(Q)]
        zt = jnp.concatenate(rows, axis=0).T.astype(BF16)
        series[e] = jnp.dot(zt[:F, :], ptab[...], preferred_element_type=F32) + jnp.dot(
            zt[F:, :], qtab[...], preferred_element_type=F32
        )
    for cp in copies:
        cp.wait()

    def finish(i, _):
        place(i).wait()
        return 0

    lax.fori_loop(0, CH, finish, 0)


def back(g, vis, z_in, ptab, qtab):
    vmem = pl.BlockSpec(memory_space=pltpu.VMEM)
    return pl.pallas_call(
        back_kernel,
        out_shape=(
            jax.ShapeDtypeStruct((CHB, 2, ROWS, A), BF16),
            jax.ShapeDtypeStruct((2, F, FL), F32),
        ),
        in_specs=[vmem] * 5,
        out_specs=(pl.BlockSpec(memory_space=pl.ANY), vmem),
        scratch_shapes=[
            pltpu.VMEM((CH, 2, ROWS, A), BF16),
            pltpu.SemaphoreType.DMA((PARTS,)),
            pltpu.SemaphoreType.DMA((CH,)),
        ],
        compiler_params=pltpu.CompilerParams(vmem_limit_bytes=BACK_VMEM),
        name="back",
    )(g, vis, z_in, ptab, qtab)


BACK_VMEM = 12 * 2**20


def body(samples, history, antenna_flags, beam_delays):
    held = front(samples, history, jnp.asarray(tap_table()), antenna_flags.reshape(NR, ROWS), beam_delays)
    return back(*held)


def solution(mesh):
    in_specs = (P(None, "chan", "row"), P(None, "chan", None), P(), P())
    out_specs = (P("chan", None, "row", None), P(("chan", "row"), None, None))
    return jax.shard_map(body, mesh=mesh, in_specs=in_specs, out_specs=out_specs, check_vma=False)
```

```python
import math

import jax
import jax.numpy as jnp
import numpy as np
from jax import lax
from jax.experimental import pallas as pl
from jax.experimental.pallas import tpu as pltpu
from jax.sharding import PartitionSpec as P

A = 1024
FL = 1024
NCH = 512
TAPS = 8
BEAMS = 256
NC = 16
NR = 8
CHB = NCH // NC
ROWS = A // NR
AL = ROWS // NC
F = 64
SIZES = (4, 8, 8, 8, 4)
Q = len(SIZES)
OFFS = tuple(sum(SIZES[:q]) for q in range(Q))
BIG = max(SIZES)
HIST = (TAPS - 1) * FL
SPAN = (F // NR) * FL
MESH = pl.DeviceIdType.MESH
F32 = jnp.float32
BF16 = jnp.bfloat16
NKIND = 9


def tap_table():
    position = (np.arange(TAPS * FL, dtype=np.int32).astype(np.float32) + np.float32(0.5)).astype(np.float64)
    centred = position / FL - TAPS / 2.0
    window = 0.5 - 0.5 * np.cos(2.0 * math.pi * position / (TAPS * FL))
    return (np.sinc(centred) * window).reshape(TAPS, FL).astype(np.float32)


def cos_sin(m):
    quarter = lax.shift_right_logical(m, 8)
    x = ((m & 255) - 128).astype(F32) * (2.0 * math.pi / FL)
    x2 = x * x
    s = x * (1.0 + x2 * (-1.0 / 6 + x2 * (1.0 / 120 + x2 * (-1.0 / 5040 + x2 * (1.0 / 362880)))))
    c = 1.0 + x2 * (-0.5 + x2 * (1.0 / 24 + x2 * (-1.0 / 720 + x2 * (1.0 / 40320 + x2 * (-1.0 / 3628800)))))
    root = math.sqrt(0.5)
    ca = (c - s) * root
    sa = (c + s) * root
    odd = (quarter & 1) == 1
    neg = quarter >= 2
    cv = jnp.where(odd, -sa, ca)
    sv = jnp.where(odd, ca, sa)
    return jnp.where(neg, -cv, cv), jnp.where(neg, -sv, sv)


def nt(lhs, rhs):
    return lax.dot_general(lhs, rhs, (((1,), (1,)), ((), ())), preferred_element_type=F32)


def gram_lhs(own):
    low = lax.broadcasted_iota(jnp.int32, (ROWS, 128), 1) < 64
    turned = pltpu.roll(own.astype(F32), 64, 1)
    return jnp.concatenate([own, jnp.where(low, turned, -turned).astype(BF16)], axis=0) * BF16(1.0 / F)


def front_kernel(
    samples, history, taps_in, flags_in, delays, vis, z_in, ptab, qtab,
    g, ext, dl, taps, flags, filt32, filt, dftc, dfts, tmp, sbuf, abuf, fl, wcos, wall, bacc, bs, bsend,
    s_row, r_row, s_loc, s_ch, r_ch, s_g, r_g, s_bm, r_bm,
):
    c = lax.axis_index("chan")
    r = lax.axis_index("row")
    h = r // 4
    z = lax.rem(r, 4)
    zp = lax.rem(z + 1, 4)
    zm = lax.rem(z + 3, 4)
    z2 = lax.rem(z + 2, 4)
    up = {"chan": c, "row": h * 4 + zp}
    dn = {"chan": c, "row": h * 4 + zm}
    over = {"chan": c, "row": (1 - h) * 4 + z}
    row_own = [h * 4 + v for v in (z, zp, z2, zm)]
    row_oth = [(1 - h) * 4 + v for v in (z, zp, z2, zm)]

    def remote(src, dst, ss, rs, dev):
        return pltpu.make_async_remote_copy(
            src_ref=src, dst_ref=dst, send_sem=ss, recv_sem=rs, device_id=dev, device_id_type=MESH
        )

    barrier = pltpu.get_barrier_semaphore()
    for d in range(1, NR):
        pl.semaphore_signal(barrier, inc=1, device_id={"chan": c, "row": lax.rem(r + d, NR)}, device_id_type=MESH)
    for d in range(1, NC):
        pl.semaphore_signal(barrier, inc=1, device_id={"chan": lax.rem(c + d, NC), "row": r}, device_id_type=MESH)

    def span(row):
        return ext.at[:, pl.ds(pl.multiple_of(HIST + row * SPAN, FL), SPAN)]

    local = [
        pltpu.make_async_copy(src, dst, s_loc.at[k])
        for k, (src, dst) in enumerate(
            (
                (samples.at[r], span(r)),
                (history.at[r], ext.at[:, pl.ds(0, HIST)]),
                (delays, dl),
                (taps_in, taps),
                (flags_in, flags),
            )
        )
    ]
    for cp in local:
        cp.start()
    pl.semaphore_wait(barrier, NR - 1 + NC - 1)

    copies = []

    def start(cp):
        cp.start()
        copies.append(cp)

    for d in (6, 7, 5, 2, 4, 1, 3):
        to = (row_own + row_oth)[d]
        start(remote(samples.at[to], span(r), s_row.at[d], r_row.at[d], {"chan": c, "row": to}))
    for q in range(Q):

        def dft_rows(i, _, q=q):
            row = i * 16 + lax.broadcasted_iota(jnp.int32, (16, FL), 0)
            k = (row // SIZES[q]) * CHB + OFFS[q] + row % SIZES[q]
            n = lax.broadcasted_iota(jnp.int32, (16, FL), 1)
            cv, sv = cos_sin((k * n) & (FL - 1))
            scale = 1.0 / math.sqrt(FL)
            at = pl.ds(pl.multiple_of(NC * OFFS[q] + i * 16, 16), 16)
            dftc[at, :] = (cv * scale).astype(BF16)
            dfts[at, :] = (-sv * scale).astype(BF16)
            return 0

        lax.fori_loop(0, SIZES[q], dft_rows, 0)

    def synth_rows(i, _):
        k = i * 16 + lax.broadcasted_iota(jnp.int32, (16, FL), 0)
        n = lax.broadcasted_iota(jnp.int32, (16, FL), 1)
        cv, sv = cos_sin((k * n) & (FL - 1))
        scale = 1.0 / math.sqrt(NCH)
        at = pl.ds(pl.multiple_of(i * 16, 16), 16)
        ptab[at, :] = (cv * scale).astype(BF16)
        qtab[at, :] = (-sv * scale).astype(BF16)
        return 0

    lax.fori_loop(0, NCH // 16, synth_rows, 0)

    local[2].wait()
    local[4].wait()
    for e in range(2):
        for i in range(NC):
            wcos[e * NC + i : e * NC + i + 1, :] = dl[pl.ds(i * 2 * NR + 2 * r + e, 1), :]

    def steer(i, _):
        lanes = pl.ds(pl.multiple_of(i * 128, 128), 128)
        d = wcos[:, lanes]
        cr, ci = cos_sin((d * (c * CHB)) & (FL - 1))
        sr, si = cos_sin(d)
        scale = 1.0 / math.sqrt(A)
        for ch in range(CHB):
            wall[ch, 0:32, lanes] = (cr * scale).astype(BF16)
            wall[ch, 32:64, lanes] = (-ci * scale).astype(BF16)
            cr, ci = cr * sr - ci * si, cr * si + ci * sr
        return 0

    lax.fori_loop(0, A // 128, steer, 0)
    fl[...] = jnp.broadcast_to(flags[pl.ds(r, 1), :].astype(F32), (ROWS, 128)).T

    local[0].wait()
    local[1].wait()
    local[3].wait()
    for d, frm in (
        (1, row_own[3]), (3, row_own[1]), (2, row_own[2]),
        (4, row_oth[0]), (5, row_oth[3]), (7, row_oth[1]), (6, row_oth[2]),
    ):
        remote(samples.at[frm], span(frm), s_row.at[d], r_row.at[d], {"chan": c, "row": frm}).wait_recv()

    def pfb(i, _):
        lanes = pl.ds(pl.multiple_of(i * 128, 128), 128)
        tap = [jnp.broadcast_to(taps[t : t + 1, lanes], (AL, 128)) for t in range(TAPS)]
        win = [ext[:, pl.ds(pl.multiple_of(t * FL + i * 128, 128), 128)].astype(F32) for t in range(TAPS - 1)]
        for f in range(F):
            win.append(ext[:, pl.ds(pl.multiple_of((f + TAPS - 1) * FL + i * 128, 128), 128)].astype(F32))
            acc = win[f] * tap[0]
            for t in range(1, TAPS):
                acc = acc + win[f + t] * tap[t]
            filt32[f * AL : (f + 1) * AL, :] = acc
        for a in range(AL):
            for b in range(F // 16):
                filt[a * F + b * 16 : a * F + (b + 1) * 16, lanes] = filt32[
                    pl.ds(b * 16 * AL + a, 16, stride=AL), :
                ].astype(BF16)
        return 0

    lax.fori_loop(0, FL // 128, pfb, 0)

    def piece(buf, dev, q):
        return buf.at[dev, pl.ds(OFFS[q] * AL, SIZES[q] * AL)]

    def spectra(q):
        size, kk = SIZES[q], NC * SIZES[q]
        low = lax.broadcasted_iota(jnp.int32, (kk, 128), 1) < 64
        rows = slice(NC * OFFS[q], NC * OFFS[q] + kk)
        re = nt(dftc[rows, :], filt[...])
        im = nt(dfts[rows, :], filt[...])
        for t in range(AL // 2):
            rt = re[:, t * 128 : (t + 1) * 128]
            it = im[:, t * 128 : (t + 1) * 128]
            tmp[(2 * t) * kk : (2 * t + 1) * kk, :] = jnp.where(low, rt, pltpu.roll(it, 64, 1))
            tmp[(2 * t + 1) * kk : (2 * t + 2) * kk, :] = jnp.where(low, pltpu.roll(rt, 64, 1), it)

        def turn(i, _):
            for p in range(size // 2):
                pair = [tmp[pl.ds(i * size + 2 * p + e, AL, stride=kk), :] for e in range(2)]
                at = OFFS[q] * AL + p * 16
                sbuf[i, at : at + 16, :] = jnp.concatenate(pair, axis=0).astype(BF16)
            return 0

        lax.fori_loop(0, NC, turn, 0)
        for d in range(1, NC):
            to = lax.rem(c + d, NC)
            start(remote(piece(sbuf, to, q), piece(abuf, c, q), s_ch.at[q, d], r_ch.at[q, d], {"chan": to, "row": r}))
        at = slice(OFFS[q] * AL, (OFFS[q] + size) * AL)
        abuf[c, at, :] = sbuf[c, at, :]

    def part(row, q, half=None):
        if half is None:
            return g.at[row, pl.ds(OFFS[q], SIZES[q])]
        return g.at[row, pl.ds(OFFS[q] + half * (SIZES[q] // 2), SIZES[q] // 2)]

    def send(q, kind, src, dst, dev):
        start(remote(src, dst, s_g.at[q, kind], r_g.at[q, kind], dev))

    def arrived(q, kind, dst, dev):
        remote(dst, dst, s_g.at[q, kind], r_g.at[q, kind], dev).wait_recv()

    def own_block(q):
        for d in range(1, NC):
            frm = lax.rem(c + NC - d, NC)
            remote(piece(sbuf, frm, q), piece(abuf, frm, q), s_ch.at[q, d], r_ch.at[q, d], {"chan": frm, "row": r}).wait_recv()
        for p in range(SIZES[q] // 2):
            at = OFFS[q] * AL + p * 16
            x = abuf[:, at : at + 16, :].astype(F32)
            for e in range(2):
                v = x[:, e * AL : (e + 1) * AL, :].reshape(ROWS, 128) * fl[...]
                g[r, OFFS[q] + 2 * p + e] = v.astype(BF16)
        send(q, 4, part(r, q), part(r, q), over)
        send(q, 0, part(r, q), part(r, q), up)
        send(q, 1, part(r, q), part(r, q), dn)

    def relay(q):
        arrived(q, 0, part(row_own[3], q), dn)
        send(q, 2, part(row_own[3], q, 0), part(row_own[3], q, 0), up)
        arrived(q, 1, part(row_own[1], q), up)
        send(q, 3, part(row_own[1], q, 1), part(row_own[1], q, 1), dn)

    def spread(q):
        arrived(q, 4, part(row_oth[0], q), over)
        send(q, 5, part(row_oth[0], q), part(row_oth[0], q), up)
        send(q, 6, part(row_oth[0], q), part(row_oth[0], q), dn)

    def cross(q):
        arrived(q, 2, part(row_own[2], q, 0), dn)
        send(q, 7, part(row_own[2], q, 0), part(row_own[2], q, 0), over)
        arrived(q, 3, part(row_own[2], q, 1), up)
        send(q, 8, part(row_own[2], q, 1), part(row_own[2], q, 1), over)

    lane = lax.broadcasted_iota(jnp.int32, (32, 128), 1) < 64

    def block(row):
        return pl.ds(pl.multiple_of(row * ROWS, ROWS), ROWS)

    def grams(ch, pair):
        both = jnp.concatenate([g[row, ch] for row in pair], axis=0)
        acc = nt(gram_lhs(g[r, ch]), both).astype(BF16)
        for k, row in enumerate(pair):
            vis[ch, 0, :, block(row)] = acc[:ROWS, k * ROWS : (k + 1) * ROWS]
            vis[ch, 1, :, block(row)] = acc[ROWS:, k * ROWS : (k + 1) * ROWS]

    def beams(ch, pair):
        w = jnp.concatenate([wall[ch, :, block(row)] for row in pair], axis=1)
        x = jnp.concatenate([g[row, ch] for row in pair], axis=0)
        return jnp.dot(w, x, preferred_element_type=F32)

    def own_plane(q):
        def one(i, _):
            ch = OFFS[q] + i
            bacc[ch] = beams(ch, row_own[:2]) + beams(ch, row_own[2:])
            grams(ch, row_own[:2])
            grams(ch, row_own[2:])
            return 0

        lax.fori_loop(0, SIZES[q], one, 0)

    def other_plane(q):
        arrived(q, 7, part(row_oth[2], q, 0), over)
        arrived(q, 8, part(row_oth[2], q, 1), over)

        def one(i, _):
            ch = OFFS[q] + i
            bacc[ch] += beams(ch, row_oth[::2])
            grams(ch, row_oth[::2])
            return 0

        lax.fori_loop(0, SIZES[q], one, 0)

    def last_rows(q):
        arrived(q, 5, part(row_oth[3], q), dn)
        arrived(q, 6, part(row_oth[1], q), up)

        for i in range(SIZES[q]):
            ch = OFFS[q] + i
            acc = bacc[ch] + beams(ch, row_oth[1::2])
            turned = pltpu.roll(acc[32:, :], 64, 1)
            bs[i * 32 : (i + 1) * 32, :] = acc[:32, :] + jnp.where(lane, -turned, turned)

        def leaf(buf, dev):
            return buf.at[dev, pl.ds(2 * OFFS[q], 2 * SIZES[q])]

        for i in range(NC):
            for e in range(2):
                at = 2 * OFFS[q] + e * SIZES[q]
                bsend[i, at : at + SIZES[q], :] = bs[pl.ds(e * 16 + i, SIZES[q], stride=32), :]
        for d in range(1, NC):
            to = lax.rem(c + d, NC)
            start(remote(leaf(bsend, to), leaf(z_in, c), s_bm.at[q, d], r_bm.at[q, d], {"chan": to, "row": r}))
        at = slice(2 * OFFS[q], 2 * (OFFS[q] + SIZES[q]))
        z_in[c, at, :] = bsend[c, at, :]

        def one(i, _):
            grams(OFFS[q] + i, row_oth[1::2])
            return 0

        lax.fori_loop(0, SIZES[q], one, 0)

    spectra(0)
    spectra(1)
    own_block(0)
    spectra(2)
    own_block(1)
    spectra(3)
    spectra(4)
    own_block(2)
    early = len(copies)
    relay(0)
    own_block(3)
    relay(1)
    own_block(4)
    relay(2)
    cross(0)
    relay(3)
    cross(1)
    relay(4)
    for q in range(Q):
        spread(q)
    for cp in copies[:early]:
        cp.wait_send()
    gathered = len(copies)
    for q in range(Q):
        own_plane(q)
        if q + 2 < Q:
            cross(q + 2)
    def collect(q):
        for d in range(1, NC):
            frm = lax.rem(c + NC - d, NC)
            at = pl.ds(2 * OFFS[q], 2 * SIZES[q])
            remote(
                bsend.at[frm, at], z_in.at[frm, at], s_bm.at[q, d], r_bm.at[q, d], {"chan": frm, "row": r}
            ).wait_recv()

    for q in range(Q):
        other_plane(q)
        if q == Q - 1:
            for cp in copies[early:gathered]:
                cp.wait_send()
        last_rows(q)
        if q >= 2:
            collect(q - 2)
    for cp in copies[gathered:]:
        cp.wait_send()
    collect(Q - 2)
    collect(Q - 1)


def front(samples, history, taps, flags, delays):
    vmem = pl.BlockSpec(memory_space=pltpu.VMEM)
    hbm = pl.BlockSpec(memory_space=pl.ANY)
    dma = pltpu.SemaphoreType.DMA
    return pl.pallas_call(
        front_kernel,
        out_shape=(
            pltpu.VMEM((CHB, 2, ROWS, A), BF16),
            pltpu.VMEM((NC, 2 * CHB, 128), F32),
            pltpu.VMEM((NCH, FL), BF16),
            pltpu.VMEM((NCH, FL), BF16),
        ),
        in_specs=[hbm] * 5,
        out_specs=(vmem,) * 4,
        scratch_shapes=[
            pltpu.VMEM((NR, CHB, ROWS, 128), BF16),
            pltpu.VMEM((AL, HIST + F * FL), BF16),
            pltpu.VMEM((BEAMS, A), jnp.int32),
            pltpu.VMEM((TAPS, FL), F32),
            pltpu.VMEM((NR, ROWS), jnp.int32),
            pltpu.VMEM((F * AL, 128), F32),
            pltpu.VMEM((F * AL, FL), BF16),
            pltpu.VMEM((NCH, FL), BF16),
            pltpu.VMEM((NCH, FL), BF16),
            pltpu.VMEM((AL * NC * BIG, 128), F32),
            pltpu.VMEM((NC, CHB * AL, 128), BF16),
            pltpu.VMEM((NC, CHB * AL, 128), BF16),
            pltpu.VMEM((ROWS, 128), F32),
            pltpu.VMEM((32, A), jnp.int32),
            pltpu.VMEM((CHB, 64, A), BF16),
            pltpu.VMEM((CHB, 64, 128), F32),
            pltpu.VMEM((BIG * 32, 128), F32),
            pltpu.VMEM((NC, 2 * CHB, 128), F32),
            dma((NR,)),
            dma((NR,)),
            dma((5,)),
            dma((Q, NC)),
            dma((Q, NC)),
            dma((Q, NKIND)),
            dma((Q, NKIND)),
            dma((Q, NC)),
            dma((Q, NC)),
        ],
        compiler_params=pltpu.CompilerParams(
            collective_id=0, has_side_effects=True, vmem_limit_bytes=FRONT_VMEM
        ),
        name="front",
    )(samples, history, taps, flags, delays)


FRONT_VMEM = 42 * 2**20
PARTS = 16


def back_kernel(vis, z_in, ptab, qtab, out, series_out, series, s_vis, s_ser):
    step = CHB // PARTS
    copies = [
        pltpu.make_async_copy(vis.at[pl.ds(i * step, step)], out.at[pl.ds(i * step, step)], s_vis.at[i])
        for i in range(PARTS)
    ]
    for cp in copies:
        cp.start()
    for e in range(2):
        rows = []
        for i in range(NC):
            for q in range(Q):
                at = 2 * OFFS[q] + e * SIZES[q]
                rows.append(z_in[i, at : at + SIZES[q], :])
        zt = jnp.concatenate(rows, axis=0).T.astype(BF16)
        series[e] = jnp.dot(zt[:F, :], ptab[...], preferred_element_type=F32) + jnp.dot(
            zt[F:, :], qtab[...], preferred_element_type=F32
        )
        cp = pltpu.make_async_copy(series.at[e], series_out.at[e], s_ser.at[e])
        cp.start()
        copies.append(cp)
    for cp in copies:
        cp.wait()


def back(vis, z_in, ptab, qtab):
    vmem = pl.BlockSpec(memory_space=pltpu.VMEM)
    return pl.pallas_call(
        back_kernel,
        out_shape=(
            jax.ShapeDtypeStruct((CHB, 2, ROWS, A), BF16),
            jax.ShapeDtypeStruct((2, F, FL), F32),
        ),
        in_specs=[vmem] * 4,
        out_specs=(pl.BlockSpec(memory_space=pl.ANY),) * 2,
        scratch_shapes=[
            pltpu.VMEM((2, F, FL), F32),
            pltpu.SemaphoreType.DMA((PARTS,)),
            pltpu.SemaphoreType.DMA((2,)),
        ],
        compiler_params=pltpu.CompilerParams(vmem_limit_bytes=BACK_VMEM),
        name="back",
    )(vis, z_in, ptab, qtab)


BACK_VMEM = 8 * 2**20


def body(samples, history, antenna_flags, beam_delays):
    held = front(samples, history, jnp.asarray(tap_table()), antenna_flags.reshape(NR, ROWS), beam_delays)
    return back(*held)


def solution(mesh):
    in_specs = (P(None, "chan", "row"), P(None, "chan", None), P(), P())
    out_specs = (P("chan", None, "row", None), P(("chan", "row"), None, None))
    return jax.shard_map(body, mesh=mesh, in_specs=in_specs, out_specs=out_specs, check_vma=False)
```

```python
import math

import jax
import jax.numpy as jnp
import numpy as np
from jax import lax
from jax.experimental import pallas as pl
from jax.experimental.pallas import tpu as pltpu
from jax.sharding import PartitionSpec as P

A = 1024
FL = 1024
NCH = 512
TAPS = 8
BEAMS = 256
NC = 16
NR = 8
CHB = NCH // NC
ROWS = A // NR
AL = ROWS // NC
F = 64
SIZES = (4, 8, 8, 4, 8)
Q = len(SIZES)
OFFS = tuple(sum(SIZES[:q]) for q in range(Q))
BIG = max(SIZES)
SHARED = 4
SH_OFF = OFFS[SHARED]
HIST = (TAPS - 1) * FL
SPAN = (F // NR) * FL
MESH = pl.DeviceIdType.MESH
F32 = jnp.float32
BF16 = jnp.bfloat16
NKIND = 10


def tap_table():
    position = (np.arange(TAPS * FL, dtype=np.int32).astype(np.float32) + np.float32(0.5)).astype(np.float64)
    centred = position / FL - TAPS / 2.0
    window = 0.5 - 0.5 * np.cos(2.0 * math.pi * position / (TAPS * FL))
    return (np.sinc(centred) * window).reshape(TAPS, FL).astype(np.float32)


def cos_sin(m):
    quarter = lax.shift_right_logical(m, 8)
    x = ((m & 255) - 128).astype(F32) * (2.0 * math.pi / FL)
    x2 = x * x
    s = x * (1.0 + x2 * (-1.0 / 6 + x2 * (1.0 / 120 + x2 * (-1.0 / 5040 + x2 * (1.0 / 362880)))))
    c = 1.0 + x2 * (-0.5 + x2 * (1.0 / 24 + x2 * (-1.0 / 720 + x2 * (1.0 / 40320 + x2 * (-1.0 / 3628800)))))
    root = math.sqrt(0.5)
    ca = (c - s) * root
    sa = (c + s) * root
    odd = (quarter & 1) == 1
    neg = quarter >= 2
    cv = jnp.where(odd, -sa, ca)
    sv = jnp.where(odd, ca, sa)
    return jnp.where(neg, -cv, cv), jnp.where(neg, -sv, sv)


def nt(lhs, rhs):
    return lax.dot_general(lhs, rhs, (((1,), (1,)), ((), ())), preferred_element_type=F32)


def gram_lhs(own):
    low = lax.broadcasted_iota(jnp.int32, (ROWS, 128), 1) < 64
    turned = pltpu.roll(own.astype(F32), 64, 1)
    return jnp.concatenate([own, jnp.where(low, turned, -turned).astype(BF16)], axis=0) * BF16(1.0 / F)


def front_kernel(
    samples, history, taps_in, flags_in, delays, vis, z_in, ptab, qtab,
    g, ext, dl, taps, flags, filt32, filt, dft, tmp, sbuf, abuf, fl, wcos, wall, wall2, pout, pin, bacc, bs, bsend,
    s_row, r_row, s_loc, s_ch, r_ch, s_g, r_g, s_bm, r_bm,
):
    c = lax.axis_index("chan")
    r = lax.axis_index("row")
    h = r // 4
    z = lax.rem(r, 4)
    zp = lax.rem(z + 1, 4)
    zm = lax.rem(z + 3, 4)
    z2 = lax.rem(z + 2, 4)
    up = {"chan": c, "row": h * 4 + zp}
    dn = {"chan": c, "row": h * 4 + zm}
    over = {"chan": c, "row": (1 - h) * 4 + z}
    row_own = [h * 4 + v for v in (z, zp, z2, zm)]
    row_oth = [(1 - h) * 4 + v for v in (z, zp, z2, zm)]

    def remote(src, dst, ss, rs, dev):
        return pltpu.make_async_remote_copy(
            src_ref=src, dst_ref=dst, send_sem=ss, recv_sem=rs, device_id=dev, device_id_type=MESH
        )

    barrier = pltpu.get_barrier_semaphore()
    for d in range(1, NR):
        pl.semaphore_signal(barrier, inc=1, device_id={"chan": c, "row": lax.rem(r + d, NR)}, device_id_type=MESH)
    for d in range(1, NC):
        pl.semaphore_signal(barrier, inc=1, device_id={"chan": lax.rem(c + d, NC), "row": r}, device_id_type=MESH)

    def span(row):
        return ext.at[:, pl.ds(pl.multiple_of(HIST + row * SPAN, FL), SPAN)]

    local = [
        pltpu.make_async_copy(src, dst, s_loc.at[k])
        for k, (src, dst) in enumerate(
            (
                (samples.at[r], span(r)),
                (history.at[r], ext.at[:, pl.ds(0, HIST)]),
                (delays, dl),
                (taps_in, taps),
                (flags_in, flags),
            )
        )
    ]
    for cp in local:
        cp.start()
    pl.semaphore_wait(barrier, NR - 1 + NC - 1)

    copies = []

    def start(cp):
        cp.start()
        copies.append(cp)

    for d in (6, 7, 5, 2, 4, 1, 3):
        to = (row_own + row_oth)[d]
        start(remote(samples.at[to], span(r), s_row.at[d], r_row.at[d], {"chan": c, "row": to}))
    for q in range(Q):

        def dft_rows(i, _, q=q):
            row = i * 16 + lax.broadcasted_iota(jnp.int32, (16, FL), 0)
            k = (row // SIZES[q]) * CHB + OFFS[q] + row % SIZES[q]
            n = lax.broadcasted_iota(jnp.int32, (16, FL), 1)
            cv, sv = cos_sin((k * n) & (FL - 1))
            scale = 1.0 / math.sqrt(FL)
            at = 2 * NC * OFFS[q] + i * 16
            dft[pl.ds(pl.multiple_of(at, 16), 16), :] = (cv * scale).astype(BF16)
            dft[pl.ds(pl.multiple_of(at + NC * SIZES[q], 16), 16), :] = (-sv * scale).astype(BF16)
            return 0

        lax.fori_loop(0, SIZES[q], dft_rows, 0)

    def synth_rows(i, _):
        k = i * 16 + lax.broadcasted_iota(jnp.int32, (16, FL), 0)
        n = lax.broadcasted_iota(jnp.int32, (16, FL), 1)
        cv, sv = cos_sin((k * n) & (FL - 1))
        scale = 1.0 / math.sqrt(NCH)
        at = pl.ds(pl.multiple_of(i * 16, 16), 16)
        ptab[at, :] = (cv * scale).astype(BF16)
        qtab[at, :] = (-sv * scale).astype(BF16)
        return 0

    lax.fori_loop(0, NCH // 16, synth_rows, 0)

    local[2].wait()
    local[4].wait()
    def steer(row, weights, first, lane0, blocks):
        for e in range(2):
            for i in range(NC):
                wcos[e * NC + i : e * NC + i + 1, :] = dl[pl.ds(i * 2 * NR + 2 * row + e, 1), :]

        def one(i, _):
            d = wcos[:, pl.ds(pl.multiple_of(lane0 + i * 128, 128), 128)]
            to = pl.ds(pl.multiple_of(i * 128, 128), 128)
            cr, ci = cos_sin((d * (c * CHB + first)) & (FL - 1))
            sr, si = cos_sin(d)
            scale = 1.0 / math.sqrt(A)
            for ch in range(CHB - first):
                weights[ch, 0:32, to] = (cr * scale).astype(BF16)
                weights[ch, 32:64, to] = (-ci * scale).astype(BF16)
                cr, ci = cr * sr - ci * si, cr * si + ci * sr
            return 0

        lax.fori_loop(0, blocks, one, 0)

    steer(r, wall, 0, 0, NR)
    steer(row_oth[0], wall2, SH_OFF, h * (A // 2), NR // 2)
    fl[...] = jnp.broadcast_to(flags[pl.ds(r, 1), :].astype(F32), (ROWS, 128)).T

    local[0].wait()
    local[1].wait()
    local[3].wait()
    for d, frm in (
        (1, row_own[3]), (3, row_own[1]), (2, row_own[2]),
        (4, row_oth[0]), (5, row_oth[3]), (7, row_oth[1]), (6, row_oth[2]),
    ):
        remote(samples.at[frm], span(frm), s_row.at[d], r_row.at[d], {"chan": c, "row": frm}).wait_recv()

    def pfb(i, _):
        lanes = pl.ds(pl.multiple_of(i * 128, 128), 128)
        tap = [jnp.broadcast_to(taps[t : t + 1, lanes], (AL, 128)) for t in range(TAPS)]
        win = [ext[:, pl.ds(pl.multiple_of(t * FL + i * 128, 128), 128)].astype(F32) for t in range(TAPS - 1)]
        for f in range(F):
            win.append(ext[:, pl.ds(pl.multiple_of((f + TAPS - 1) * FL + i * 128, 128), 128)].astype(F32))
            acc = win[f] * tap[0]
            for t in range(1, TAPS):
                acc = acc + win[f + t] * tap[t]
            filt32[f * AL : (f + 1) * AL, :] = acc
        for a in range(AL):
            for b in range(F // 16):
                filt[a * F + b * 16 : a * F + (b + 1) * 16, lanes] = filt32[
                    pl.ds(b * 16 * AL + a, 16, stride=AL), :
                ].astype(BF16)
        return 0

    lax.fori_loop(0, FL // 128, pfb, 0)

    def piece(buf, dev, q):
        return buf.at[dev, pl.ds(OFFS[q] * AL, SIZES[q] * AL)]

    def spectra(q):
        size, kk = SIZES[q], NC * SIZES[q]
        low = lax.broadcasted_iota(jnp.int32, (kk, 128), 1) < 64
        both = nt(dft[2 * NC * OFFS[q] : 2 * NC * OFFS[q] + 2 * kk, :], filt[...])
        re, im = both[:kk], both[kk:]
        for t in range(AL // 2):
            rt = re[:, t * 128 : (t + 1) * 128]
            it = im[:, t * 128 : (t + 1) * 128]
            tmp[(2 * t) * kk : (2 * t + 1) * kk, :] = jnp.where(low, rt, pltpu.roll(it, 64, 1))
            tmp[(2 * t + 1) * kk : (2 * t + 2) * kk, :] = jnp.where(low, pltpu.roll(rt, 64, 1), it)

        def turn(i, _):
            for p in range(size // 2):
                pair = [tmp[pl.ds(i * size + 2 * p + e, AL, stride=kk), :] for e in range(2)]
                at = OFFS[q] * AL + p * 16
                sbuf[i, at : at + 16, :] = jnp.concatenate(pair, axis=0).astype(BF16)
            return 0

        lax.fori_loop(0, NC, turn, 0)
        for d in range(1, NC):
            to = lax.rem(c + d, NC)
            start(remote(piece(sbuf, to, q), piece(abuf, c, q), s_ch.at[q, d], r_ch.at[q, d], {"chan": to, "row": r}))
        at = slice(OFFS[q] * AL, (OFFS[q] + size) * AL)
        abuf[c, at, :] = sbuf[c, at, :]

    def part(row, q, half=None):
        if half is None:
            return g.at[row, pl.ds(OFFS[q], SIZES[q])]
        return g.at[row, pl.ds(OFFS[q] + half * (SIZES[q] // 2), SIZES[q] // 2)]

    def send(q, kind, src, dst, dev):
        start(remote(src, dst, s_g.at[q, kind], r_g.at[q, kind], dev))

    def arrived(q, kind, dst, dev):
        remote(dst, dst, s_g.at[q, kind], r_g.at[q, kind], dev).wait_recv()

    def own_block(q):
        for d in range(1, NC):
            frm = lax.rem(c + NC - d, NC)
            remote(piece(sbuf, frm, q), piece(abuf, frm, q), s_ch.at[q, d], r_ch.at[q, d], {"chan": frm, "row": r}).wait_recv()
        for p in range(SIZES[q] // 2):
            at = OFFS[q] * AL + p * 16
            x = abuf[:, at : at + 16, :].astype(F32)
            for e in range(2):
                v = x[:, e * AL : (e + 1) * AL, :].reshape(ROWS, 128) * fl[...]
                g[r, OFFS[q] + 2 * p + e] = v.astype(BF16)
        send(q, 4, part(r, q), part(r, q), over)
        send(q, 0, part(r, q), part(r, q), up)
        send(q, 1, part(r, q), part(r, q), dn)

    def relay(q):
        arrived(q, 0, part(row_own[3], q), dn)
        send(q, 2, part(row_own[3], q, 0), part(row_own[3], q, 0), up)
        arrived(q, 1, part(row_own[1], q), up)
        send(q, 3, part(row_own[1], q, 1), part(row_own[1], q, 1), dn)

    def spread(q):
        arrived(q, 4, part(row_oth[0], q), over)
        send(q, 5, part(row_oth[0], q), part(row_oth[0], q), up)
        send(q, 6, part(row_oth[0], q), part(row_oth[0], q), dn)

    lane = lax.broadcasted_iota(jnp.int32, (32, 128), 1) < 64

    def joined(acc):
        turned = pltpu.roll(acc[32:, :], 64, 1)
        return acc[:32, :] + jnp.where(lane, -turned, turned)

    def shared(q, buf):
        return buf.at[pl.ds(OFFS[q] - SH_OFF, SIZES[q])]

    def cross(q):
        arrived(q, 2, part(row_own[2], q, 0), dn)
        arrived(q, 3, part(row_own[2], q, 1), up)
        if q >= SHARED:
            for i in range(SIZES[q]):
                ch = OFFS[q] + i
                x = jnp.concatenate([g[h * 4 + v, ch] for v in range(4)], axis=0)
                pout[ch - SH_OFF] = joined(jnp.dot(wall2[ch - SH_OFF], x, preferred_element_type=F32)).astype(BF16)
            send(q, 9, shared(q, pout), shared(q, pin), over)
        send(q, 7, part(row_own[2], q, 0), part(row_own[2], q, 0), over)
        send(q, 8, part(row_own[2], q, 1), part(row_own[2], q, 1), over)

    def block(row):
        return pl.ds(pl.multiple_of(row * ROWS, ROWS), ROWS)

    def grams(ch, pair):
        both = jnp.concatenate([g[row, ch] for row in pair], axis=0)
        acc = nt(gram_lhs(g[r, ch]), both).astype(BF16)
        for k, row in enumerate(pair):
            vis[ch, 0, :, block(row)] = acc[:ROWS, k * ROWS : (k + 1) * ROWS]
            vis[ch, 1, :, block(row)] = acc[ROWS:, k * ROWS : (k + 1) * ROWS]

    def beams(ch, pair):
        w = jnp.concatenate([wall[ch, :, block(row)] for row in pair], axis=1)
        x = jnp.concatenate([g[row, ch] for row in pair], axis=0)
        return jnp.dot(w, x, preferred_element_type=F32)

    def own_plane(q):
        def one(i, _):
            ch = OFFS[q] + i
            bacc[ch] = beams(ch, row_own[:2]) + beams(ch, row_own[2:])
            grams(ch, row_own[:2])
            grams(ch, row_own[2:])
            return 0

        lax.fori_loop(0, SIZES[q], one, 0)

    def other_plane(q):
        arrived(q, 7, part(row_oth[2], q, 0), over)
        arrived(q, 8, part(row_oth[2], q, 1), over)

        def one(i, _):
            ch = OFFS[q] + i
            if q < SHARED:
                bacc[ch] += beams(ch, row_oth[::2])
            grams(ch, row_oth[::2])
            return 0

        lax.fori_loop(0, SIZES[q], one, 0)

    def send_beams(q):
        if q >= SHARED:
            arrived(q, 9, shared(q, pin), over)
        for i in range(SIZES[q]):
            ch = OFFS[q] + i
            if q >= SHARED:
                beam = joined(bacc[ch]) + pin[ch - SH_OFF].astype(F32)
            else:
                beam = joined(bacc[ch] + beams(ch, row_oth[1::2]))
            bs[i * 32 : (i + 1) * 32, :] = beam

        def leaf(buf, dev):
            return buf.at[dev, pl.ds(2 * OFFS[q], 2 * SIZES[q])]

        for i in range(NC):
            for e in range(2):
                at = 2 * OFFS[q] + e * SIZES[q]
                bsend[i, at : at + SIZES[q], :] = bs[pl.ds(e * 16 + i, SIZES[q], stride=32), :]
        for d in range(1, NC):
            to = lax.rem(c + d, NC)
            start(remote(leaf(bsend, to), leaf(z_in, c), s_bm.at[q, d], r_bm.at[q, d], {"chan": to, "row": r}))
        at = slice(2 * OFFS[q], 2 * (OFFS[q] + SIZES[q]))
        z_in[c, at, :] = bsend[c, at, :]

    def last_rows(q):
        arrived(q, 5, part(row_oth[3], q), dn)
        arrived(q, 6, part(row_oth[1], q), up)
        if q < SHARED:
            send_beams(q)

        def one(i, _):
            grams(OFFS[q] + i, row_oth[1::2])
            return 0

        lax.fori_loop(0, SIZES[q], one, 0)

    spectra(0)
    spectra(1)
    own_block(0)
    spectra(2)
    own_block(1)
    spectra(3)
    spectra(4)
    own_block(2)
    early = len(copies)
    relay(0)
    own_block(3)
    relay(1)
    own_block(4)
    relay(2)
    cross(0)
    relay(3)
    cross(1)
    relay(4)
    for q in range(Q):
        spread(q)
    for cp in copies[:early]:
        cp.wait_send()
    gathered = len(copies)
    for q in range(Q):
        own_plane(q)
        if q + 2 < Q:
            cross(q + 2)
    def collect(q):
        for d in range(1, NC):
            frm = lax.rem(c + NC - d, NC)
            at = pl.ds(2 * OFFS[q], 2 * SIZES[q])
            remote(
                bsend.at[frm, at], z_in.at[frm, at], s_bm.at[q, d], r_bm.at[q, d], {"chan": frm, "row": r}
            ).wait_recv()

    for q in range(SHARED):
        other_plane(q)
        last_rows(q)
    for q in range(SHARED, Q):
        send_beams(q)
        other_plane(q)
        for k in range(3):
            collect(k)
        if q == Q - 1:
            for cp in copies[early:gathered]:
                cp.wait_send()
        last_rows(q)
    for cp in copies[gathered:]:
        cp.wait_send()
    collect(3)
    collect(4)


def front(samples, history, taps, flags, delays):
    vmem = pl.BlockSpec(memory_space=pltpu.VMEM)
    hbm = pl.BlockSpec(memory_space=pl.ANY)
    dma = pltpu.SemaphoreType.DMA
    return pl.pallas_call(
        front_kernel,
        out_shape=(
            pltpu.VMEM((CHB, 2, ROWS, A), BF16),
            pltpu.VMEM((NC, 2 * CHB, 128), F32),
            pltpu.VMEM((NCH, FL), BF16),
            pltpu.VMEM((NCH, FL), BF16),
        ),
        in_specs=[hbm] * 5,
        out_specs=(vmem,) * 4,
        scratch_shapes=[
            pltpu.VMEM((NR, CHB, ROWS, 128), BF16),
            pltpu.VMEM((AL, HIST + F * FL), BF16),
            pltpu.VMEM((BEAMS, A), jnp.int32),
            pltpu.VMEM((TAPS, FL), F32),
            pltpu.VMEM((NR, ROWS), jnp.int32),
            pltpu.VMEM((F * AL, 128), F32),
            pltpu.VMEM((F * AL, FL), BF16),
            pltpu.VMEM((2 * NCH, FL), BF16),
            pltpu.VMEM((AL * NC * BIG, 128), F32),
            pltpu.VMEM((NC, CHB * AL, 128), BF16),
            pltpu.VMEM((NC, CHB * AL, 128), BF16),
            pltpu.VMEM((ROWS, 128), F32),
            pltpu.VMEM((32, A), jnp.int32),
            pltpu.VMEM((CHB, 64, A), BF16),
            pltpu.VMEM((CHB - SH_OFF, 64, A // 2), BF16),
            pltpu.VMEM((CHB - SH_OFF, 32, 128), BF16),
            pltpu.VMEM((CHB - SH_OFF, 32, 128), BF16),
            pltpu.VMEM((CHB, 64, 128), F32),
            pltpu.VMEM((BIG * 32, 128), F32),
            pltpu.VMEM((NC, 2 * CHB, 128), F32),
            dma((NR,)),
            dma((NR,)),
            dma((5,)),
            dma((Q, NC)),
            dma((Q, NC)),
            dma((Q, NKIND)),
            dma((Q, NKIND)),
            dma((Q, NC)),
            dma((Q, NC)),
        ],
        compiler_params=pltpu.CompilerParams(
            collective_id=0, has_side_effects=True, vmem_limit_bytes=FRONT_VMEM
        ),
        name="front",
    )(samples, history, taps, flags, delays)


FRONT_VMEM = 42 * 2**20
PARTS = 16


def back_kernel(vis, z_in, ptab, qtab, out, series_out, series, s_vis, s_ser):
    step = CHB // PARTS
    copies = [
        pltpu.make_async_copy(vis.at[pl.ds(i * step, step)], out.at[pl.ds(i * step, step)], s_vis.at[i])
        for i in range(PARTS)
    ]
    for cp in copies:
        cp.start()
    for e in range(2):
        rows = []
        for i in range(NC):
            for q in range(Q):
                at = 2 * OFFS[q] + e * SIZES[q]
                rows.append(z_in[i, at : at + SIZES[q], :])
        zt = jnp.concatenate(rows, axis=0).T.astype(BF16)
        series[e] = jnp.dot(zt[:F, :], ptab[...], preferred_element_type=F32) + jnp.dot(
            zt[F:, :], qtab[...], preferred_element_type=F32
        )
        cp = pltpu.make_async_copy(series.at[e], series_out.at[e], s_ser.at[e])
        cp.start()
        copies.append(cp)
    for cp in copies:
        cp.wait()


def back(vis, z_in, ptab, qtab):
    vmem = pl.BlockSpec(memory_space=pltpu.VMEM)
    return pl.pallas_call(
        back_kernel,
        out_shape=(
            jax.ShapeDtypeStruct((CHB, 2, ROWS, A), BF16),
            jax.ShapeDtypeStruct((2, F, FL), F32),
        ),
        in_specs=[vmem] * 4,
        out_specs=(pl.BlockSpec(memory_space=pl.ANY),) * 2,
        scratch_shapes=[
            pltpu.VMEM((2, F, FL), F32),
            pltpu.SemaphoreType.DMA((PARTS,)),
            pltpu.SemaphoreType.DMA((2,)),
        ],
        compiler_params=pltpu.CompilerParams(vmem_limit_bytes=BACK_VMEM),
        name="back",
    )(vis, z_in, ptab, qtab)


BACK_VMEM = 8 * 2**20


def body(samples, history, antenna_flags, beam_delays):
    held = front(samples, history, jnp.asarray(tap_table()), antenna_flags.reshape(NR, ROWS), beam_delays)
    return back(*held)


def solution(mesh):
    in_specs = (P(None, "chan", "row"), P(None, "chan", None), P(), P())
    out_specs = (P("chan", None, "row", None), P(("chan", "row"), None, None))
    return jax.shard_map(body, mesh=mesh, in_specs=in_specs, out_specs=out_specs, check_vma=False)
```

```python
import math

import jax
import jax.numpy as jnp
import numpy as np
from jax import lax
from jax.experimental import pallas as pl
from jax.experimental.pallas import tpu as pltpu
from jax.sharding import PartitionSpec as P

A = 1024
FL = 1024
NCH = 512
TAPS = 8
BEAMS = 256
NC = 16
NR = 8
CHB = NCH // NC
ROWS = A // NR
AL = ROWS // NC
F = 64
SIZES = (4, 8, 8, 4, 8)
Q = len(SIZES)
OFFS = tuple(sum(SIZES[:q]) for q in range(Q))
BIG = max(SIZES)
SHARED = 4
SH_OFF = OFFS[SHARED]
HIST = (TAPS - 1) * FL
SPAN = (F // NR) * FL
MESH = pl.DeviceIdType.MESH
F32 = jnp.float32
BF16 = jnp.bfloat16
NKIND = 10


def tap_table():
    position = (np.arange(TAPS * FL, dtype=np.int32).astype(np.float32) + np.float32(0.5)).astype(np.float64)
    centred = position / FL - TAPS / 2.0
    window = 0.5 - 0.5 * np.cos(2.0 * math.pi * position / (TAPS * FL))
    return (np.sinc(centred) * window).reshape(TAPS, FL).astype(np.float32)


def cos_sin(m):
    quarter = lax.shift_right_logical(m, 8)
    x = ((m & 255) - 128).astype(F32) * (2.0 * math.pi / FL)
    x2 = x * x
    s = x * (1.0 + x2 * (-1.0 / 6 + x2 * (1.0 / 120 + x2 * (-1.0 / 5040 + x2 * (1.0 / 362880)))))
    c = 1.0 + x2 * (-0.5 + x2 * (1.0 / 24 + x2 * (-1.0 / 720 + x2 * (1.0 / 40320 + x2 * (-1.0 / 3628800)))))
    root = math.sqrt(0.5)
    ca = (c - s) * root
    sa = (c + s) * root
    odd = (quarter & 1) == 1
    neg = quarter >= 2
    cv = jnp.where(odd, -sa, ca)
    sv = jnp.where(odd, ca, sa)
    return jnp.where(neg, -cv, cv), jnp.where(neg, -sv, sv)


def nt(lhs, rhs):
    return lax.dot_general(lhs, rhs, (((1,), (1,)), ((), ())), preferred_element_type=F32)


def gram_lhs(own):
    low = lax.broadcasted_iota(jnp.int32, (ROWS, 128), 1) < 64
    turned = pltpu.roll(own.astype(F32), 64, 1)
    return jnp.concatenate([own, jnp.where(low, turned, -turned).astype(BF16)], axis=0) * BF16(1.0 / F)


def front_kernel(
    samples, history, taps_in, flags_in, delays, vis, z_in, ptab, qtab,
    g, ext, dl, taps, flags, filt32, filt, dft, tmp, sbuf, abuf, fl, wcos, wall, wall2, pout, pin, bacc, bs, bsend,
    s_row, r_row, s_loc, s_ch, r_ch, s_g, r_g, s_bm, r_bm,
):
    c = lax.axis_index("chan")
    r = lax.axis_index("row")
    h = r // 4
    z = lax.rem(r, 4)
    zp = lax.rem(z + 1, 4)
    zm = lax.rem(z + 3, 4)
    z2 = lax.rem(z + 2, 4)
    up = {"chan": c, "row": h * 4 + zp}
    dn = {"chan": c, "row": h * 4 + zm}
    over = {"chan": c, "row": (1 - h) * 4 + z}
    row_own = [h * 4 + v for v in (z, zp, z2, zm)]
    row_oth = [(1 - h) * 4 + v for v in (z, zp, z2, zm)]

    def remote(src, dst, ss, rs, dev):
        return pltpu.make_async_remote_copy(
            src_ref=src, dst_ref=dst, send_sem=ss, recv_sem=rs, device_id=dev, device_id_type=MESH
        )

    barrier = pltpu.get_barrier_semaphore()
    for d in range(1, NR):
        pl.semaphore_signal(barrier, inc=1, device_id={"chan": c, "row": lax.rem(r + d, NR)}, device_id_type=MESH)
    for d in range(1, NC):
        pl.semaphore_signal(barrier, inc=1, device_id={"chan": lax.rem(c + d, NC), "row": r}, device_id_type=MESH)

    def span(row):
        return ext.at[:, pl.ds(pl.multiple_of(HIST + row * SPAN, FL), SPAN)]

    local = [
        pltpu.make_async_copy(src, dst, s_loc.at[k])
        for k, (src, dst) in enumerate(
            (
                (samples.at[r], span(r)),
                (history.at[r], ext.at[:, pl.ds(0, HIST)]),
                (delays, dl),
                (taps_in, taps),
                (flags_in, flags),
            )
        )
    ]
    for cp in local:
        cp.start()
    pl.semaphore_wait(barrier, NR - 1 + NC - 1)

    copies = []

    def start(cp):
        cp.start()
        copies.append(cp)

    for d in (6, 7, 5, 2, 4, 1, 3):
        to = (row_own + row_oth)[d]
        start(remote(samples.at[to], span(r), s_row.at[d], r_row.at[d], {"chan": c, "row": to}))
    for q in range(Q):

        def dft_rows(i, _, q=q):
            row = i * 16 + lax.broadcasted_iota(jnp.int32, (16, FL), 0)
            k = (row // SIZES[q]) * CHB + OFFS[q] + row % SIZES[q]
            n = lax.broadcasted_iota(jnp.int32, (16, FL), 1)
            cv, sv = cos_sin((k * n) & (FL - 1))
            scale = 1.0 / math.sqrt(FL)
            at = 2 * NC * OFFS[q] + i * 16
            dft[pl.ds(pl.multiple_of(at, 16), 16), :] = (cv * scale).astype(BF16)
            dft[pl.ds(pl.multiple_of(at + NC * SIZES[q], 16), 16), :] = (-sv * scale).astype(BF16)
            return 0

        lax.fori_loop(0, SIZES[q], dft_rows, 0)

    def synth_rows(i, _):
        k = i * 16 + lax.broadcasted_iota(jnp.int32, (16, FL), 0)
        n = lax.broadcasted_iota(jnp.int32, (16, FL), 1)
        cv, sv = cos_sin((k * n) & (FL - 1))
        scale = 1.0 / math.sqrt(NCH)
        at = pl.ds(pl.multiple_of(i * 16, 16), 16)
        ptab[at, :] = (cv * scale).astype(BF16)
        qtab[at, :] = (-sv * scale).astype(BF16)
        return 0

    lax.fori_loop(0, NCH // 16, synth_rows, 0)

    local[2].wait()
    local[4].wait()
    def steer(row, weights, first, lane0, blocks):
        for e in range(2):
            for i in range(NC):
                wcos[e * NC + i : e * NC + i + 1, :] = dl[pl.ds(i * 2 * NR + 2 * row + e, 1), :]

        def one(i, _):
            d = wcos[:, pl.ds(pl.multiple_of(lane0 + i * 128, 128), 128)]
            to = pl.ds(pl.multiple_of(i * 128, 128), 128)
            cr, ci = cos_sin((d * (c * CHB + first)) & (FL - 1))
            sr, si = cos_sin(d)
            scale = 1.0 / math.sqrt(A)
            for ch in range(CHB - first):
                weights[ch, 0:32, to] = (cr * scale).astype(BF16)
                weights[ch, 32:64, to] = (-ci * scale).astype(BF16)
                cr, ci = cr * sr - ci * si, cr * si + ci * sr
            return 0

        lax.fori_loop(0, blocks, one, 0)

    steer(r, wall, 0, 0, NR)
    steer(row_oth[0], wall2, SH_OFF, h * (A // 2), NR // 2)
    fl[...] = jnp.broadcast_to(flags[pl.ds(r, 1), :].astype(F32), (ROWS, 128)).T

    local[0].wait()
    local[1].wait()
    local[3].wait()
    for d, frm in (
        (1, row_own[3]), (3, row_own[1]), (2, row_own[2]),
        (4, row_oth[0]), (5, row_oth[3]), (7, row_oth[1]), (6, row_oth[2]),
    ):
        remote(samples.at[frm], span(frm), s_row.at[d], r_row.at[d], {"chan": c, "row": frm}).wait_recv()

    def pfb(i, _):
        lanes = pl.ds(pl.multiple_of(i * 128, 128), 128)
        tap = [jnp.broadcast_to(taps[t : t + 1, lanes], (AL, 128)) for t in range(TAPS)]
        win = [ext[:, pl.ds(pl.multiple_of(t * FL + i * 128, 128), 128)].astype(F32) for t in range(TAPS - 1)]
        for f in range(F):
            win.append(ext[:, pl.ds(pl.multiple_of((f + TAPS - 1) * FL + i * 128, 128), 128)].astype(F32))
            acc = win[f] * tap[0]
            for t in range(1, TAPS):
                acc = acc + win[f + t] * tap[t]
            filt32[f * AL : (f + 1) * AL, :] = acc
        for a in range(AL):
            for b in range(F // 16):
                filt[a * F + b * 16 : a * F + (b + 1) * 16, lanes] = filt32[
                    pl.ds(b * 16 * AL + a, 16, stride=AL), :
                ].astype(BF16)
        return 0

    lax.fori_loop(0, FL // 128, pfb, 0)

    def piece(buf, dev, q):
        return buf.at[dev, pl.ds(OFFS[q] * AL, SIZES[q] * AL)]

    def spectra(q):
        size, kk = SIZES[q], NC * SIZES[q]
        low = lax.broadcasted_iota(jnp.int32, (kk, 128), 1) < 64
        both = nt(dft[2 * NC * OFFS[q] : 2 * NC * OFFS[q] + 2 * kk, :], filt[...])
        re, im = both[:kk], both[kk:]
        for t in range(AL // 2):
            rt = re[:, t * 128 : (t + 1) * 128]
            it = im[:, t * 128 : (t + 1) * 128]
            tmp[(2 * t) * kk : (2 * t + 1) * kk, :] = jnp.where(low, rt, pltpu.roll(it, 64, 1))
            tmp[(2 * t + 1) * kk : (2 * t + 2) * kk, :] = jnp.where(low, pltpu.roll(rt, 64, 1), it)

        def turn(i, _):
            for p in range(size // 2):
                pair = [tmp[pl.ds(i * size + 2 * p + e, AL, stride=kk), :] for e in range(2)]
                at = OFFS[q] * AL + p * 16
                sbuf[i, at : at + 16, :] = jnp.concatenate(pair, axis=0).astype(BF16)
            return 0

        lax.fori_loop(0, NC, turn, 0)
        for d in range(1, NC):
            to = lax.rem(c + d, NC)
            start(remote(piece(sbuf, to, q), piece(abuf, c, q), s_ch.at[q, d], r_ch.at[q, d], {"chan": to, "row": r}))
        at = slice(OFFS[q] * AL, (OFFS[q] + size) * AL)
        abuf[c, at, :] = sbuf[c, at, :]

    def part(row, q, half=None):
        if half is None:
            return g.at[row, pl.ds(OFFS[q], SIZES[q])]
        return g.at[row, pl.ds(OFFS[q] + half * (SIZES[q] // 2), SIZES[q] // 2)]

    def send(q, kind, src, dst, dev):
        start(remote(src, dst, s_g.at[q, kind], r_g.at[q, kind], dev))

    def arrived(q, kind, dst, dev):
        remote(dst, dst, s_g.at[q, kind], r_g.at[q, kind], dev).wait_recv()

    def own_block(q):
        for d in range(1, NC):
            frm = lax.rem(c + NC - d, NC)
            remote(piece(sbuf, frm, q), piece(abuf, frm, q), s_ch.at[q, d], r_ch.at[q, d], {"chan": frm, "row": r}).wait_recv()
        for p in range(SIZES[q] // 2):
            at = OFFS[q] * AL + p * 16
            x = abuf[:, at : at + 16, :].astype(F32)
            for e in range(2):
                v = x[:, e * AL : (e + 1) * AL, :].reshape(ROWS, 128) * fl[...]
                g[r, OFFS[q] + 2 * p + e] = v.astype(BF16)
        send(q, 4, part(r, q), part(r, q), over)
        send(q, 0, part(r, q), part(r, q), up)
        send(q, 1, part(r, q), part(r, q), dn)

    def relay(q):
        arrived(q, 0, part(row_own[3], q), dn)
        send(q, 2, part(row_own[3], q, 0), part(row_own[3], q, 0), up)
        arrived(q, 1, part(row_own[1], q), up)
        send(q, 3, part(row_own[1], q, 1), part(row_own[1], q, 1), dn)

    def spread(q):
        arrived(q, 4, part(row_oth[0], q), over)
        send(q, 5, part(row_oth[0], q), part(row_oth[0], q), up)
        send(q, 6, part(row_oth[0], q), part(row_oth[0], q), dn)

    lane = lax.broadcasted_iota(jnp.int32, (32, 128), 1) < 64

    def joined(acc):
        turned = pltpu.roll(acc[32:, :], 64, 1)
        return acc[:32, :] + jnp.where(lane, -turned, turned)

    def shared(q, buf):
        return buf.at[pl.ds(OFFS[q] - SH_OFF, SIZES[q])]

    def cross(q):
        arrived(q, 2, part(row_own[2], q, 0), dn)
        arrived(q, 3, part(row_own[2], q, 1), up)
        if q >= SHARED:
            for i in range(SIZES[q]):
                ch = OFFS[q] + i
                x = jnp.concatenate([g[h * 4 + v, ch] for v in range(4)], axis=0)
                pout[ch - SH_OFF] = joined(jnp.dot(wall2[ch - SH_OFF], x, preferred_element_type=F32)).astype(BF16)
            send(q, 9, shared(q, pout), shared(q, pin), over)
        send(q, 7, part(row_own[2], q, 0), part(row_own[2], q, 0), over)
        send(q, 8, part(row_own[2], q, 1), part(row_own[2], q, 1), over)

    def block(row):
        return pl.ds(pl.multiple_of(row * ROWS, ROWS), ROWS)

    def grams(ch, pair):
        both = jnp.concatenate([g[row, ch] for row in pair], axis=0)
        acc = nt(gram_lhs(g[r, ch]), both).astype(BF16)
        for k, row in enumerate(pair):
            vis[ch, 0, :, block(row)] = acc[:ROWS, k * ROWS : (k + 1) * ROWS]
            vis[ch, 1, :, block(row)] = acc[ROWS:, k * ROWS : (k + 1) * ROWS]

    def beams(ch, pair):
        w = jnp.concatenate([wall[ch, :, block(row)] for row in pair], axis=1)
        x = jnp.concatenate([g[row, ch] for row in pair], axis=0)
        return jnp.dot(w, x, preferred_element_type=F32)

    def own_plane(q):
        def one(i, _):
            ch = OFFS[q] + i
            bacc[ch] = beams(ch, row_own[:2]) + beams(ch, row_own[2:])
            grams(ch, row_own[:2])
            grams(ch, row_own[2:])
            return 0

        lax.fori_loop(0, SIZES[q], one, 0)

    def other_plane(q):
        arrived(q, 7, part(row_oth[2], q, 0), over)
        arrived(q, 8, part(row_oth[2], q, 1), over)

        def one(i, _):
            ch = OFFS[q] + i
            if q < SHARED:
                bacc[ch] += beams(ch, row_oth[::2])
            grams(ch, row_oth[::2])
            return 0

        lax.fori_loop(0, SIZES[q], one, 0)

    def send_beams(q):
        if q >= SHARED:
            arrived(q, 9, shared(q, pin), over)
        for i in range(SIZES[q]):
            ch = OFFS[q] + i
            if q >= SHARED:
                beam = joined(bacc[ch]) + pin[ch - SH_OFF].astype(F32)
            else:
                beam = joined(bacc[ch] + beams(ch, row_oth[1::2]))
            bs[i * 32 : (i + 1) * 32, :] = beam

        def leaf(buf, dev):
            return buf.at[dev, pl.ds(2 * OFFS[q], 2 * SIZES[q])]

        for i in range(NC):
            for e in range(2):
                at = 2 * OFFS[q] + e * SIZES[q]
                bsend[i, at : at + SIZES[q], :] = bs[pl.ds(e * 16 + i, SIZES[q], stride=32), :]
        for d in range(1, NC):
            to = lax.rem(c + d, NC)
            start(remote(leaf(bsend, to), leaf(z_in, c), s_bm.at[q, d], r_bm.at[q, d], {"chan": to, "row": r}))
        at = slice(2 * OFFS[q], 2 * (OFFS[q] + SIZES[q]))
        z_in[c, at, :] = bsend[c, at, :]

    def last_rows(q):
        arrived(q, 5, part(row_oth[3], q), dn)
        arrived(q, 6, part(row_oth[1], q), up)
        if q < SHARED:
            send_beams(q)

        def one(i, _):
            grams(OFFS[q] + i, row_oth[1::2])
            return 0

        lax.fori_loop(0, SIZES[q], one, 0, unroll=q == Q - 1)

    spectra(0)
    spectra(1)
    own_block(0)
    spectra(2)
    own_block(1)
    spectra(3)
    spectra(4)
    own_block(2)
    early = len(copies)
    relay(0)
    own_block(3)
    relay(1)
    own_block(4)
    relay(2)
    cross(0)
    relay(3)
    cross(1)
    relay(4)
    for q in range(Q):
        spread(q)
    for cp in copies[:early]:
        cp.wait_send()
    gathered = len(copies)
    for q in range(Q):
        own_plane(q)
        if q + 2 < Q:
            cross(q + 2)
    def collect(q):
        for d in range(1, NC):
            frm = lax.rem(c + NC - d, NC)
            at = pl.ds(2 * OFFS[q], 2 * SIZES[q])
            remote(
                bsend.at[frm, at], z_in.at[frm, at], s_bm.at[q, d], r_bm.at[q, d], {"chan": frm, "row": r}
            ).wait_recv()

    for q in range(SHARED):
        other_plane(q)
        last_rows(q)
    for q in range(SHARED, Q):
        send_beams(q)
        other_plane(q)
        for k in range(3):
            collect(k)
        if q == Q - 1:
            for cp in copies[early:gathered]:
                cp.wait_send()
        last_rows(q)
    for cp in copies[gathered:]:
        cp.wait_send()
    collect(3)
    collect(4)


def front(samples, history, taps, flags, delays):
    vmem = pl.BlockSpec(memory_space=pltpu.VMEM)
    hbm = pl.BlockSpec(memory_space=pl.ANY)
    dma = pltpu.SemaphoreType.DMA
    return pl.pallas_call(
        front_kernel,
        out_shape=(
            pltpu.VMEM((CHB, 2, ROWS, A), BF16),
            pltpu.VMEM((NC, 2 * CHB, 128), F32),
            pltpu.VMEM((NCH, FL), BF16),
            pltpu.VMEM((NCH, FL), BF16),
        ),
        in_specs=[hbm] * 5,
        out_specs=(vmem,) * 4,
        scratch_shapes=[
            pltpu.VMEM((NR, CHB, ROWS, 128), BF16),
            pltpu.VMEM((AL, HIST + F * FL), BF16),
            pltpu.VMEM((BEAMS, A), jnp.int32),
            pltpu.VMEM((TAPS, FL), F32),
            pltpu.VMEM((NR, ROWS), jnp.int32),
            pltpu.VMEM((F * AL, 128), F32),
            pltpu.VMEM((F * AL, FL), BF16),
            pltpu.VMEM((2 * NCH, FL), BF16),
            pltpu.VMEM((AL * NC * BIG, 128), F32),
            pltpu.VMEM((NC, CHB * AL, 128), BF16),
            pltpu.VMEM((NC, CHB * AL, 128), BF16),
            pltpu.VMEM((ROWS, 128), F32),
            pltpu.VMEM((32, A), jnp.int32),
            pltpu.VMEM((CHB, 64, A), BF16),
            pltpu.VMEM((CHB - SH_OFF, 64, A // 2), BF16),
            pltpu.VMEM((CHB - SH_OFF, 32, 128), BF16),
            pltpu.VMEM((CHB - SH_OFF, 32, 128), BF16),
            pltpu.VMEM((CHB, 64, 128), F32),
            pltpu.VMEM((BIG * 32, 128), F32),
            pltpu.VMEM((NC, 2 * CHB, 128), F32),
            dma((NR,)),
            dma((NR,)),
            dma((5,)),
            dma((Q, NC)),
            dma((Q, NC)),
            dma((Q, NKIND)),
            dma((Q, NKIND)),
            dma((Q, NC)),
            dma((Q, NC)),
        ],
        compiler_params=pltpu.CompilerParams(
            collective_id=0, has_side_effects=True, vmem_limit_bytes=FRONT_VMEM
        ),
        name="front",
    )(samples, history, taps, flags, delays)


FRONT_VMEM = 42 * 2**20
PARTS = 16


def back_kernel(vis, z_in, ptab, qtab, out, series_out, series, s_vis, s_ser):
    step = CHB // PARTS
    copies = [
        pltpu.make_async_copy(vis.at[pl.ds(i * step, step)], out.at[pl.ds(i * step, step)], s_vis.at[i])
        for i in range(PARTS)
    ]
    for cp in copies:
        cp.start()
    for e in range(2):
        rows = []
        for i in range(NC):
            for q in range(Q):
                at = 2 * OFFS[q] + e * SIZES[q]
                rows.append(z_in[i, at : at + SIZES[q], :])
        zt = jnp.concatenate(rows, axis=0).T.astype(BF16)
        series[e] = jnp.dot(zt[:F, :], ptab[...], preferred_element_type=F32) + jnp.dot(
            zt[F:, :], qtab[...], preferred_element_type=F32
        )
        cp = pltpu.make_async_copy(series.at[e], series_out.at[e], s_ser.at[e])
        cp.start()
        copies.append(cp)
    for cp in copies:
        cp.wait()


def back(vis, z_in, ptab, qtab):
    vmem = pl.BlockSpec(memory_space=pltpu.VMEM)
    return pl.pallas_call(
        back_kernel,
        out_shape=(
            jax.ShapeDtypeStruct((CHB, 2, ROWS, A), BF16),
            jax.ShapeDtypeStruct((2, F, FL), F32),
        ),
        in_specs=[vmem] * 4,
        out_specs=(pl.BlockSpec(memory_space=pl.ANY),) * 2,
        scratch_shapes=[
            pltpu.VMEM((2, F, FL), F32),
            pltpu.SemaphoreType.DMA((PARTS,)),
            pltpu.SemaphoreType.DMA((2,)),
        ],
        compiler_params=pltpu.CompilerParams(vmem_limit_bytes=BACK_VMEM),
        name="back",
    )(vis, z_in, ptab, qtab)


BACK_VMEM = 8 * 2**20


def body(samples, history, antenna_flags, beam_delays):
    held = front(samples, history, jnp.asarray(tap_table()), antenna_flags.reshape(NR, ROWS), beam_delays)
    return back(*held)


def solution(mesh):
    in_specs = (P(None, "chan", "row"), P(None, "chan", None), P(), P())
    out_specs = (P("chan", None, "row", None), P(("chan", "row"), None, None))
    return jax.shard_map(body, mesh=mesh, in_specs=in_specs, out_specs=out_specs, check_vma=False)
```
